32 devices in a mesh: tp: 4 (over x, core), sp: 8 (over z, y).
Axes of the slice: x: 2, y: 2, z: 4, core: 2. Of those that a mesh axis runs over, the one named last changes fastest.
Arguments:
- tokens: bfloat16 [16384, 768], P('sp'), may hold values from -6 to 6
- condition: float32 [4, 768], replicated, may hold values from -6 to 6
- clip_ids: int32 [64], replicated, may hold values from 0 to 3, as said below
- w_mod: bfloat16 [768, 6912], P('sp'), may hold values from -0.21875 to 0.21875
- w_qkv_s: bfloat16 [3, 768, 768], P(None, 'sp', 'tp'), may hold values from -0.21875 to 0.21875
- w_o_s: bfloat16 [768, 768], P('tp', 'sp'), may hold values from -2.5 to 2.5
- w_qkv_t: bfloat16 [3, 768, 768], P(None, 'sp', 'tp'), may hold values from -0.21875 to 0.21875
- w_o_t: bfloat16 [768, 768], P('tp', 'sp'), may hold values from -0.875 to 0.875
- w_up: bfloat16 [768, 3072], P('sp', 'tp'), may hold values from -0.21875 to 0.21875
- w_down: bfloat16 [3072, 768], P('tp', 'sp'), may hold values from -0.109375 to 0.109375
- grad_out: bfloat16 [16384, 768], P('sp'), may hold values from -6 to 6
Outputs:
- block_out: bfloat16 [16384, 768], P('sp')
- grad_tokens: bfloat16 [16384, 768], P('sp')
- grad_condition: float32 [4, 768], replicated
- grad_w_mod: float32 [768, 6912], P('sp')
- grad_w_qkv_s: float32 [3, 768, 768], P(None, 'sp', 'tp')
- grad_w_o_s: float32 [768, 768], P('tp', 'sp')
- grad_w_qkv_t: float32 [3, 768, 768], P(None, 'sp', 'tp')
- grad_w_o_t: float32 [768, 768], P('tp', 'sp')
- grad_w_up: float32 [768, 3072], P('sp', 'tp')
- grad_w_down: float32 [3072, 768], P('tp', 'sp')
The draws below stay inside these ranges and needn't reach their ends.
Inputs may be any that keep to these rules, and one draw needn't show every extreme that they name: `clip_ids`: each of the 4 clips holds 1 to 32 frames, which need not be consecutive, and one holds exactly 32; the first and the last frame belong to the same clip.
All inputs are finite; a program needn't handle non-finite values.
Results may differ from the reference program's by a relative error of at most 0.025.
Values may be sent and summed in bfloat16 or wider, within the bound.
No kernel may reach another device: no remote copies, remote signals or barrier semaphores. Data moves between devices by JAX's collectives and lax.ppermute only.
A program may use at most 256 MiB of HBM per device.

```python
import math
from functools import partial
import jax
import jax.numpy as jnp
from jax import lax

D = 768
HEADS = 12
HD = 64
FF = 3072
PATCHES = 256
NF = 64
TOKENS = 16384
CLIPS = 4
MAXLEN = 32
HL = 3
FF_TP = 768


def draw_clip_ids(key, part):
    key_longest = jax.random.fold_in(key, 11)
    key_offset = jax.random.fold_in(key, 12)
    key_order = jax.random.fold_in(key, 13)
    longest = jax.random.randint(key_longest, (), 0, CLIPS, dtype=jnp.int32)
    offset = jax.random.randint(key_offset, (), 0, CLIPS - 1, dtype=jnp.int32)
    others = CLIPS - 1
    surplus = NF - MAXLEN - others
    indices = jnp.concatenate([jnp.arange(others, dtype=jnp.int32), (jnp.arange(surplus, dtype=jnp.int32) + offset) % others])
    mapped = jnp.where(indices < longest, indices, indices + 1).astype(jnp.int32)
    remaining = jnp.concatenate([jnp.full((MAXLEN - 2,), 1, jnp.int32) * longest, mapped])
    middle = jax.random.permutation(key_order, remaining)
    return jnp.concatenate([longest[None], middle, longest[None]]).astype(jnp.int32)


def level_of(rng, dims, cuts, smallest, largest):
    gain, own = 1.0, jax.random.fold_in(rng, 6)
    for axis_at, blocks in cuts:
        steps = jnp.exp(jax.random.uniform(jax.random.fold_in(own, axis_at), (blocks,), jnp.float32, smallest / len(cuts), largest / len(cuts)))
        gain = gain * jnp.repeat(steps, dims[axis_at] // blocks).reshape([-1 if axis == axis_at else 1 for axis in range(len(dims))])
    return gain


def gaussian(rng, extent, deviation, reach, cuts=(), kind=jnp.bfloat16):
    drawn = deviation * jax.random.normal(rng, extent, jnp.float32)
    if cuts:
        drawn = drawn * level_of(rng, extent, cuts, -0.22, 0.18)
    return jnp.clip(drawn, -reach, reach).astype(kind)


def setup_inputs(seed: int = 0) -> dict:
    key_of = jax.random.split(jax.random.key(seed), 12)
    return {
        "tokens": gaussian(key_of[0], (TOKENS, D), 1.0, 6.0, ((0, 8),)),
        "condition": gaussian(key_of[1], (CLIPS, D), 1.0, 6.0, (), jnp.float32),
        "clip_ids": draw_clip_ids(jax.random.fold_in(key_of[11], 71), 0),
        "w_mod": gaussian(key_of[3], (D, 9 * D), D ** -0.5, 0.21875, ((0, 8),)),
        "w_qkv_s": gaussian(key_of[4], (3, D, D), D ** -0.5, 0.21875, ((1, 8), (2, 4))),
        "w_o_s": gaussian(key_of[5], (D, D), (D * 2 // PATCHES) ** -0.5, 2.5, ((0, 4), (1, 8))),
        "w_qkv_t": gaussian(key_of[6], (3, D, D), D ** -0.5, 0.21875, ((1, 8), (2, 4))),
        "w_o_t": gaussian(key_of[7], (D, D), (D // 16) ** -0.5, 0.875, ((0, 4), (1, 8))),
        "w_up": gaussian(key_of[8], (D, FF), D ** -0.5, 0.21875, ((0, 8), (1, 4))),
        "w_down": gaussian(key_of[9], (FF, D), FF ** -0.5, 0.109375, ((0, 4), (1, 8))),
        "grad_out": gaussian(key_of[10], (TOKENS, D), 1.0, 6.0, ((0, 8),)),
    }


EPSILON = 1e-06
HIGHEST_PRECISION = lax.Precision.HIGHEST

@jax.custom_vjp
def low(v):
    return lax.optimization_barrier(v.astype(jnp.bfloat16)).astype(jnp.float32)

@jax.custom_vjp
def low_back(v):
    return v

def low_keep(v):
    return (low(v), None)

def low_pass(kept, grad):
    return (grad,)

def back_keep(v):
    return (v, None)

def back_low(kept, grad):
    return (low(grad),)
low.defvjp(low_keep, low_pass)
low_back.defvjp(back_keep, back_low)

def norm_rows(operand):
    row_mean = lax.optimization_barrier(jnp.mean(operand, axis=-1, keepdims=True))
    centred = operand - row_mean
    return centred * lax.rsqrt(lax.optimization_barrier(jnp.mean(centred * centred, axis=-1, keepdims=True)) + EPSILON)

def project(operand, matrix):
    return jnp.einsum('fpd,de->fpe', operand, matrix, precision=HIGHEST_PRECISION)

def group_sum(operand, matrix, group_width):
    summed = jnp.zeros(operand.shape[:-1] + (matrix.shape[1],), jnp.float32)
    for group_no in range(operand.shape[-1] // group_width):
        first_col = group_no * group_width
        summed = summed + low(project(operand[..., first_col:first_col + group_width], matrix[first_col:first_col + group_width]))
    return summed

def spatial_block(block_in):
    queries, key_rows, value_rows = block_in
    raw = jnp.einsum('aqhe,akhe->ahqk', queries, key_rows, precision=HIGHEST_PRECISION) * 0.125
    scores = low_back(raw)
    weights = low(jax.nn.softmax(scores, axis=-1))
    return jnp.einsum('ahqk,akhe->aqhe', weights, value_rows, precision=HIGHEST_PRECISION)

def temporal_block(block_in, same_clip):
    queries, key_rows, value_rows = block_in
    raw = jnp.einsum('qahe,kahe->ahqk', queries, key_rows, precision=HIGHEST_PRECISION) * 0.125
    scores = jnp.where(same_clip, low_back(raw), -1e+30)
    weights = low(jax.nn.softmax(scores, axis=-1))
    return jnp.einsum('ahqk,kahe->qahe', weights, value_rows, precision=HIGHEST_PRECISION)

def heads_of(entered, w_qkv):
    return [low(low_back(project(entered, w_qkv[member]))).reshape(NF, PATCHES, HEADS, HD) for member in range(3)]

def spatial_layer(residual, mod_shift, mod_scale, mod_gate, w_qkv, w_out):
    entered = low(norm_rows(residual) * (1.0 + mod_scale) + mod_shift)
    blocks = math.gcd(NF, 16)
    grouped = [projected.reshape(NF // blocks, blocks, PATCHES, HEADS, HD) for projected in heads_of(entered, w_qkv)]
    mix_out = lax.map(jax.checkpoint(spatial_block), tuple(grouped))
    attended = low(low_back(mix_out.reshape(NF, PATCHES, D)))
    branch = low_back(group_sum(attended, w_out, HL * HD))
    return residual + mod_gate * branch

def temporal_layer(residual, mod_shift, mod_scale, mod_gate, w_qkv, w_out, same_clip):
    entered = low(norm_rows(residual) * (1.0 + mod_scale) + mod_shift)
    blocks = math.gcd(PATCHES, 16)
    grouped = [jnp.moveaxis(projected.reshape(NF, PATCHES // blocks, blocks, HEADS, HD), 1, 0) for projected in heads_of(entered, w_qkv)]
    mix_out = lax.map(jax.checkpoint(partial(temporal_block, same_clip=same_clip)), tuple(grouped))
    attended = low(low_back(jnp.moveaxis(mix_out, 0, 1).reshape(NF, PATCHES, D)))
    branch = low_back(group_sum(attended, w_out, HL * HD))
    return residual + mod_gate * branch

def feed_layer(residual, mod_shift, mod_scale, mod_gate, w_up, w_down):
    entered = low(norm_rows(residual) * (1.0 + mod_scale) + mod_shift)
    pre_act = low_back(project(entered, w_up))
    activated = low(jax.nn.gelu(pre_act, approximate=True))
    branch = low_back(group_sum(activated, w_down, FF_TP))
    return residual + mod_gate * branch

def forward(tokens, condition, w_mod, w_qkv_s, w_o_s, w_qkv_t, w_o_t, w_up, w_down, clip_ids):
    modulation = low_back(jnp.dot(low(jax.nn.silu(condition)), w_mod, precision=HIGHEST_PRECISION))
    per_frame = modulation[clip_ids][:, None, :]
    mod_parts = [per_frame[:, :, member * D:(member + 1) * D] for member in range(9)]
    same_clip = clip_ids[:, None] == clip_ids[None, :]
    residual = tokens.reshape(NF, PATCHES, D)
    residual = jax.checkpoint(spatial_layer)(residual, mod_parts[0], mod_parts[1], mod_parts[2], w_qkv_s, w_o_s)
    residual = jax.checkpoint(partial(temporal_layer, same_clip=same_clip))(residual, mod_parts[3], mod_parts[4], mod_parts[5], w_qkv_t, w_o_t)
    residual = jax.checkpoint(feed_layer)(residual, mod_parts[6], mod_parts[7], mod_parts[8], w_up, w_down)
    return residual.reshape(NF * PATCHES, D)

def reference(tokens, condition, clip_ids, w_mod, w_qkv_s, w_o_s, w_qkv_t, w_o_t, w_up, w_down, grad_out):

    def wrapped(tok_in, cond_in, mod_in, qs_in, os_in, qt_in, ot_in, up_in, down_in):
        return forward(tok_in, cond_in, mod_in, qs_in, os_in, qt_in, ot_in, up_in, down_in, clip_ids)
    result, pullback = jax.vjp(wrapped, tokens.astype(jnp.float32), condition.astype(jnp.float32), w_mod.astype(jnp.float32), w_qkv_s.astype(jnp.float32), w_o_s.astype(jnp.float32), w_qkv_t.astype(jnp.float32), w_o_t.astype(jnp.float32), w_up.astype(jnp.float32), w_down.astype(jnp.float32))
    gradients = pullback(grad_out.astype(jnp.float32))
    return (result.astype(jnp.bfloat16), gradients[0].astype(jnp.bfloat16), gradients[1], gradients[2], gradients[3], gradients[4], gradients[5], gradients[6], gradients[7], gradients[8])
```

```python
import jax
import jax.numpy as jnp
from jax import lax
from jax.sharding import PartitionSpec as P

HD = 64
PATCHES = 256
BLOCK_ROWS = 256
EPSILON = 1e-06
HIGHEST = lax.Precision.HIGHEST
BF = jnp.bfloat16
F32 = jnp.float32


def bits_of(size):
    return size.bit_length() - 1


def swap(value, axis, bit):
    size = lax.axis_size(axis)
    return lax.ppermute(value, axis, [(i, i ^ (1 << bit)) for i in range(size)])


def my_bit(axis, bit):
    return (lax.axis_index(axis) >> bit) & 1


def cube_sum(value, dims):
    for axis, bit in dims:
        value = value + swap(value, axis, bit)
    return value


def cube_gather(block, dims):
    held = block[None]
    for axis, bit in dims:
        other = swap(held, axis, bit)
        high = my_bit(axis, bit) == 1
        held = jnp.concatenate([jnp.where(high, other, held), jnp.where(high, held, other)])
    return held


def cube_scatter(parts, dims):
    for axis, bit in reversed(dims):
        half = parts.shape[0] // 2
        mine = my_bit(axis, bit)
        send = lax.dynamic_slice_in_dim(parts, (1 - mine) * half, half)
        keep = lax.dynamic_slice_in_dim(parts, mine * half, half)
        got = swap(send, axis, bit)
        parts = keep.astype(F32) + got.astype(F32)
        if half > 1:
            parts = parts.astype(BF)
    return parts[0]


def cube_dims(order):
    return [("sp", bit) for bit in order[0]] + order[1]


def in_device_order(gathered, dims, back=False):
    count = len(dims)
    want = [("tp", b) for b in reversed(range(bits_of(lax.axis_size("tp"))))]
    want += [("sp", b) for b in reversed(range(bits_of(lax.axis_size("sp"))))]
    have = list(reversed(dims))
    tail = gathered.shape[1:]
    if back:
        have, want = want, have
    split = gathered.reshape((2,) * count + tail)
    order = [have.index(w) for w in want]
    split = split.transpose(order + [count + i for i in range(len(tail))])
    return split.reshape((2**count,) + tail)


def norm_rows(operand):
    centred = operand - jnp.mean(operand, axis=-1, keepdims=True)
    inverse = lax.rsqrt(jnp.mean(centred * centred, axis=-1, keepdims=True) + EPSILON)
    return (centred * inverse, inverse)


def norm_back(incoming, normed, inverse):
    first_mean = jnp.mean(incoming, axis=-1, keepdims=True)
    second_mean = jnp.mean(incoming * normed, axis=-1, keepdims=True)
    return inverse * (incoming - first_mean - normed * second_mean)


def gelu_tanh(operand):
    return jax.nn.gelu(operand, approximate=True)


def mm(form, left, right):
    return jnp.einsum(form, left, right, preferred_element_type=F32)


def attend(qkv, mask):
    heads = qkv.reshape(qkv.shape[0], qkv.shape[1], 3, -1, HD)
    q, k, v = heads[:, :, 0], heads[:, :, 1], heads[:, :, 2]
    scores = mm("aqhe,akhe->ahqk", q, k) * 0.125
    if mask is not None:
        scores = jnp.where(mask, scores, -1e30)
    lse = jax.nn.logsumexp(scores, axis=-1, keepdims=True)
    weights = jnp.exp(scores - lse).astype(BF)
    out = mm("ahqk,akhe->aqhe", weights, v).astype(BF)
    return out.reshape(qkv.shape[0], qkv.shape[1], -1), lse


def attend_back(qkv, lse, grad, mask):
    heads = qkv.reshape(qkv.shape[0], qkv.shape[1], 3, -1, HD)
    q, k, v = heads[:, :, 0], heads[:, :, 1], heads[:, :, 2]
    grad = grad.reshape(q.shape)
    scores = mm("aqhe,akhe->ahqk", q, k) * 0.125
    if mask is not None:
        scores = jnp.where(mask, scores, -1e30)
    prob = jnp.exp(scores - lse)
    grad_p = mm("aqhe,akhe->ahqk", grad, v)
    grad_v = mm("ahqk,aqhe->akhe", prob.astype(BF), grad)
    rows = jnp.sum(prob * grad_p, axis=-1, keepdims=True)
    grad_s = (prob * (grad_p - rows)).astype(BF)
    grad_q = mm("ahqk,akhe->aqhe", grad_s, k) * 0.125
    grad_k = mm("ahqk,aqhe->akhe", grad_s, q) * 0.125
    out = jnp.stack([grad_q, grad_k, grad_v], axis=2).astype(BF)
    return out.reshape(qkv.shape)


def shards(
    tokens, condition, clip_ids, w_mod, w_qkv_s, w_o_s, w_qkv_t, w_o_t, w_up, w_down, grad_out
):
    n_tp, n_sp = lax.axis_size("tp"), lax.axis_size("sp")
    devices = n_tp * n_sp
    my_tp, my_sp = lax.axis_index("tp"), lax.axis_index("sp")
    width = tokens.shape[1]
    sp_frames = tokens.shape[0] // PATCHES
    frames = sp_frames // n_tp
    all_frames = sp_frames * n_sp
    places = PATCHES // devices
    per_block = max(1, min(places, BLOCK_ROWS // all_frames))
    blocks = places // per_block
    rows = all_frames * per_block
    clips = condition.shape[0]
    unit_tp = w_up.shape[1]
    head_tp = w_o_s.shape[0]
    row_sp = w_up.shape[0]

    sp_bits = bits_of(n_sp)
    tp_bits = bits_of(n_tp)
    far_sp = [("sp", b) for b in reversed(range(1, sp_bits))]
    dims_s = far_sp + [("sp", 0), ("tp", 1), ("tp", 0)]
    dims_t = far_sp + [("tp", 1), ("sp", 0), ("tp", 0)]
    every = [("tp", b) for b in range(tp_bits)] + [("sp", b) for b in range(sp_bits)]

    def pack(w_qkv, w_o):
        flat = w_qkv.transpose(1, 0, 2).reshape(row_sp, -1)
        return jnp.concatenate([flat, w_o.T], axis=1)

    def unpack(gathered, dims):
        full = in_device_order(gathered, dims).reshape(n_tp, width, 4, head_tp)
        full = full.transpose(1, 2, 0, 3).reshape(width, 4 * width)
        return full[:, : 3 * width], full[:, 3 * width :]

    cond_act = jax.nn.silu(condition).astype(BF)
    cond_rows = lax.dynamic_slice_in_dim(cond_act, my_sp * row_sp, row_sp, axis=1)
    modulation = cube_sum(
        jnp.dot(cond_rows, w_mod, preferred_element_type=F32),
        [("sp", b) for b in range(sp_bits)],
    )
    qkv_s, out_s = unpack(cube_gather(pack(w_qkv_s, w_o_s), dims_s), dims_s)
    qkv_t, out_t = unpack(cube_gather(pack(w_qkv_t, w_o_t), dims_t), dims_t)
    feed = lax.all_gather(jnp.stack([w_up, w_down.T]), ("tp", "sp"), axis=0)
    feed = feed.reshape(n_tp, n_sp, 2, row_sp, unit_tp).transpose(2, 0, 1, 3, 4)
    feed = feed.reshape(2, n_tp, width, unit_tp)
    up, down = feed[0], feed[1]

    hot_all = clip_ids[:, None] == jnp.arange(clips, dtype=jnp.int32)[None, :]
    first = my_sp * sp_frames + my_tp * frames
    hot_frames = lax.dynamic_slice_in_dim(hot_all, first, frames).astype(F32)
    mod_frames = jnp.dot(hot_frames, modulation, precision=HIGHEST)[:, None, :]
    mod_s = [mod_frames[:, :, i * width : (i + 1) * width] for i in range(3)]
    row_ids = jnp.repeat(clip_ids, per_block)
    mod_rows = jnp.dot(
        jnp.repeat(hot_all, per_block, axis=0).astype(F32), modulation, precision=HIGHEST
    )[None]
    mod_t = [mod_rows[:, :, i * width : (i + 1) * width] for i in range(9)]
    key = row_ids * per_block + jnp.tile(jnp.arange(per_block, dtype=jnp.int32), all_frames)
    mask = key[:, None] == key[None, :]

    def to_places(value):
        split = value.reshape(frames, devices, blocks, per_block, width).transpose(1, 2, 0, 3, 4)
        got = lax.all_to_all(split, ("sp", "tp"), 0, 0, tiled=True)
        return got.transpose(1, 0, 2, 3, 4).reshape(blocks, rows, width)

    def to_frames(value):
        split = value.reshape(blocks, devices, frames, per_block, width).transpose(1, 0, 2, 3, 4)
        got = lax.all_to_all(split, ("sp", "tp"), 0, 0, tiled=True)
        return got.transpose(2, 0, 1, 3, 4).reshape(frames, PATCHES, width)

    def input_to_places(value):
        split = value.reshape(sp_frames, n_sp, n_tp, blocks, per_block, width)
        split = lax.dynamic_slice_in_dim(split, my_tp, 1, axis=2)[:, :, 0]
        got = lax.all_to_all(split.transpose(1, 2, 0, 3, 4), "sp", 0, 0, tiled=True)
        return got.transpose(1, 0, 2, 3, 4).reshape(blocks, rows, width)

    def places_to_output(value):
        split = value.reshape(blocks, n_sp, sp_frames, per_block, width).transpose(1, 0, 2, 3, 4)
        got = lax.all_to_all(split, "sp", 0, 0, tiled=True)
        got = lax.all_gather(got, "tp", axis=0)
        return got.transpose(3, 1, 0, 2, 4, 5).reshape(-1, width)

    grad_rows = input_to_places(grad_out).astype(F32)

    own = lax.dynamic_slice_in_dim(tokens, my_tp * frames * PATCHES, frames * PATCHES)
    res0 = own.astype(F32).reshape(frames, PATCHES, width)
    n1, r1 = norm_rows(res0)
    h1 = (n1 * (1.0 + mod_s[1]) + mod_s[0]).astype(BF)
    qkv1 = mm("frd,de->fre", h1, qkv_s).astype(BF)
    o1, lse1 = attend(qkv1, None)
    a1 = mm("fre,de->frd", o1, out_s)
    x1_frames = res0 + mod_s[2] * a1
    x1 = to_places(x1_frames.astype(BF)).astype(F32)

    n2, r2 = norm_rows(x1)
    h2 = (n2 * (1.0 + mod_t[4]) + mod_t[3]).astype(BF)
    qkv2 = mm("brd,de->bre", h2, qkv_t).astype(BF)
    o2, lse2 = attend(qkv2, mask)
    a2 = mm("bre,de->brd", o2, out_t)
    x2 = x1 + mod_t[5] * a2
    n3, r3 = norm_rows(x2)
    h3 = (n3 * (1.0 + mod_t[7]) + mod_t[6]).astype(BF)

    da3 = (mod_t[8] * grad_rows).astype(BF)
    u = mm("brd,tdh->tbrh", h3, up)
    g32, gelu_pull = jax.vjp(gelu_tanh, u)
    g = g32.astype(BF)
    a3 = mm("tbrh,tdh->brd", g, down)
    dg = mm("brd,tdh->tbrh", da3, down)
    du = gelu_pull(dg)[0].astype(BF)
    grad_down = mm("brd,tbrh->tdh", da3, g).astype(BF)
    grad_up = mm("brd,tbrh->tdh", h3, du).astype(BF)
    dh3 = mm("tbrh,tdh->brd", du, up)
    block_out = places_to_output((x2 + mod_t[8] * a3).astype(BF))
    feed_grad = jnp.stack([grad_up, grad_down], axis=2).reshape(
        n_tp, n_sp, row_sp, 2, unit_tp
    )
    feed_grad = lax.psum_scatter(
        feed_grad.reshape(devices, row_sp, 2, unit_tp), ("tp", "sp"), scatter_dimension=0
    ).astype(F32)

    hot_rows = jnp.repeat(hot_all, per_block, axis=0).astype(BF)

    def clip_sum(value):
        return mm("rc,brd->cd", hot_rows, value.astype(BF))

    dm = [None] * 9
    dm[8] = clip_sum(grad_rows * a3)
    dm[6] = clip_sum(dh3)
    dm[7] = clip_sum(dh3 * n3)
    dx2 = grad_rows + norm_back(dh3 * (1.0 + mod_t[7]), n3, r3)

    dm[5] = clip_sum(dx2 * a2)
    da2 = (mod_t[5] * dx2).astype(BF)
    grad_ot = mm("brd,bre->de", da2, o2)
    do2 = mm("brd,de->bre", da2, out_t).astype(BF)
    dqkv2 = attend_back(qkv2, lse2, do2, mask)
    grad_qt = mm("brd,bre->de", h2, dqkv2)
    dh2 = mm("bre,de->brd", dqkv2, qkv_t)
    dm[3] = clip_sum(dh2)
    dm[4] = clip_sum(dh2 * n2)
    dx1 = dx2 + norm_back(dh2 * (1.0 + mod_t[4]), n2, r2)

    def scatter_grads(grad_q, grad_o, dims):
        both = jnp.concatenate([grad_q.astype(BF), grad_o.astype(BF)], axis=1)
        both = both.reshape(n_sp, row_sp, 4, n_tp, head_tp).transpose(3, 0, 1, 2, 4)
        both = both.reshape(devices, row_sp, 4 * head_tp)
        mine = cube_scatter(in_device_order(both, dims, back=True), dims)
        mine = mine.reshape(row_sp, 4, head_tp)
        return mine[:, :3].transpose(1, 0, 2), mine[:, 3].T

    sum_qt, sum_ot = scatter_grads(grad_qt, grad_ot, dims_t)
    dx1_frames = to_frames(dx1.astype(BF)).astype(F32)

    frame_sum = [None] * 3
    frame_sum[2] = jnp.sum(dx1_frames * a1, axis=1)
    da1 = (mod_s[2] * dx1_frames).astype(BF)
    grad_os = mm("frd,fre->de", da1, o1)
    do1 = mm("frd,de->fre", da1, out_s).astype(BF)
    dqkv1 = attend_back(qkv1, lse1, do1, None)
    grad_qs = mm("frd,fre->de", h1, dqkv1)
    dh1 = mm("fre,de->frd", dqkv1, qkv_s)
    frame_sum[0] = jnp.sum(dh1, axis=1)
    frame_sum[1] = jnp.sum(dh1 * n1, axis=1)
    dx0 = dx1_frames + norm_back(dh1 * (1.0 + mod_s[1]), n1, r1)
    sum_qs, sum_os = scatter_grads(grad_qs, grad_os, dims_s)
    grad_tokens = lax.all_gather(
        dx0.reshape(-1, width).astype(BF), "tp", axis=0, tiled=True
    )

    dm_s = jnp.dot(hot_frames.T, jnp.concatenate(frame_sum, axis=-1), precision=HIGHEST)
    dm_t = cube_sum(jnp.concatenate(dm[3:], axis=-1), every)
    dm_s = cube_sum(dm_s, every)
    dm_low = jnp.concatenate([dm_s, dm_t], axis=-1).astype(BF)
    grad_mod = jnp.dot(cond_rows.T, dm_low, preferred_element_type=F32)
    grad_act = jnp.dot(dm_low, w_mod.T, preferred_element_type=F32)
    sp_dims = [("sp", b) for b in range(sp_bits)]
    grad_act = cube_gather(grad_act, sp_dims).transpose(1, 0, 2).reshape(clips, width)
    unused, silu_pull = jax.vjp(jax.nn.silu, condition)
    grad_condition = silu_pull(grad_act)[0]
    return (
        block_out,
        grad_tokens,
        grad_condition,
        grad_mod,
        sum_qs,
        sum_os,
        sum_qt,
        sum_ot,
        feed_grad[:, 0],
        feed_grad[:, 1].T,
    )


def solution(mesh):
    placed = (
        P("sp", None),
        P(),
        P(),
        P("sp", None),
        P(None, "sp", "tp"),
        P("tp", "sp"),
        P(None, "sp", "tp"),
        P("tp", "sp"),
        P("sp", "tp"),
        P("tp", "sp"),
        P("sp", None),
    )
    return jax.shard_map(
        shards,
        mesh=mesh,
        in_specs=placed,
        out_specs=(
            P("sp", None),
            P("sp", None),
            P(),
            P("sp", None),
            P(None, "sp", "tp"),
            P("tp", "sp"),
            P(None, "sp", "tp"),
            P("tp", "sp"),
            P("sp", "tp"),
            P("tp", "sp"),
        ),
        check_vma=False,
    )
```

```python
import functools

import jax
import jax.numpy as jnp
from jax import lax
from jax.experimental import pallas as pl
from jax.experimental.pallas import tpu as pltpu
from jax.sharding import PartitionSpec as P

HD = 64
PATCHES = 256
BLOCK_ROWS = 256
EPSILON = 1e-06
HIGHEST = lax.Precision.HIGHEST
BF = jnp.bfloat16
F32 = jnp.float32


def bits_of(size):
    return size.bit_length() - 1


def swap(value, axis, bit):
    size = lax.axis_size(axis)
    return lax.ppermute(value, axis, [(i, i ^ (1 << bit)) for i in range(size)])


def my_bit(axis, bit):
    return (lax.axis_index(axis) >> bit) & 1


def cube_sum(value, dims):
    for axis, bit in dims:
        value = value + swap(value, axis, bit)
    return value


def cube_gather(block, dims):
    held = block[None]
    for axis, bit in dims:
        other = swap(held, axis, bit)
        high = my_bit(axis, bit) == 1
        held = jnp.concatenate([jnp.where(high, other, held), jnp.where(high, held, other)])
    return held


def cube_scatter(parts, dims):
    for axis, bit in reversed(dims):
        half = parts.shape[0] // 2
        mine = my_bit(axis, bit)
        send = lax.dynamic_slice_in_dim(parts, (1 - mine) * half, half)
        keep = lax.dynamic_slice_in_dim(parts, mine * half, half)
        got = swap(send, axis, bit)
        parts = keep.astype(F32) + got.astype(F32)
        if half > 1:
            parts = parts.astype(BF)
    return parts[0]


def cube_dims(order):
    return [("sp", bit) for bit in order[0]] + order[1]


def in_device_order(gathered, dims, back=False):
    count = len(dims)
    want = [("tp", b) for b in reversed(range(bits_of(lax.axis_size("tp"))))]
    want += [("sp", b) for b in reversed(range(bits_of(lax.axis_size("sp"))))]
    have = list(reversed(dims))
    tail = gathered.shape[1:]
    if back:
        have, want = want, have
    split = gathered.reshape((2,) * count + tail)
    order = [have.index(w) for w in want]
    split = split.transpose(order + [count + i for i in range(len(tail))])
    return split.reshape((2**count,) + tail)


VMEM_BYTES = 52 * 1024 * 1024


def near_gather(block, dims):
    held = block[None]
    for axis, bit in dims[:-1]:
        held = jnp.concatenate([held, swap(held, axis, bit)])
    return held, swap(held, *dims[-1])


def near_scatter(low, high, dims):
    got = swap(high, *dims[-1])
    for axis, bit in reversed(dims[:-1]):
        half = low.shape[0] // 2
        total = low.astype(F32) + got.astype(F32)
        low, high = total[:half].astype(BF), total[half:].astype(BF)
        got = swap(high, axis, bit)
    return (low.astype(F32) + got.astype(F32))[0]


def dims_masks(dims):
    masks = []
    for m in range(2 ** len(dims)):
        flip = {"tp": 0, "sp": 0}
        for place, (axis, bit) in enumerate(dims):
            flip[axis] |= ((m >> place) & 1) << bit
        masks.append((flip["tp"], flip["sp"]))
    return masks


def dot(left, right, left_dim, right_dim):
    return lax.dot_general(
        left, right, (((left_dim,), (right_dim,)), ((), ())), preferred_element_type=F32
    )


def norm_rows(operand):
    centred = operand - jnp.mean(operand, axis=-1, keepdims=True)
    inverse = lax.rsqrt(jnp.mean(centred * centred, axis=-1, keepdims=True) + EPSILON)
    return (centred * inverse, inverse)


def norm_back(incoming, normed, inverse):
    first_mean = jnp.mean(incoming, axis=-1, keepdims=True)
    second_mean = jnp.mean(incoming * normed, axis=-1, keepdims=True)
    return inverse * (incoming - first_mean - normed * second_mean)


def params(count=1):
    return pltpu.CompilerParams(
        dimension_semantics=("arbitrary",) * count, vmem_limit_bytes=VMEM_BYTES
    )


def whole(shape):
    zeros = (0,) * len(shape)
    return pl.BlockSpec(shape, lambda g, meta: zeros, pipeline_mode=pl.Buffered(1))


def place_weights(meta, pieces, masks, target):
    if masks is None:
        target[...] = pieces[0][...]
        return
    rows = pieces[0].shape[1]
    half = pieces[0].shape[0]
    for m, (tp_flip, sp_flip) in enumerate(masks):
        at = pl.multiple_of((meta[2] ^ sp_flip) * rows, rows)
        target[meta[1] ^ tp_flip, pl.ds(at, rows), :] = pieces[m // half][m % half]


def forward_kernel(masks, heads, masked, meta, x, hot, mst, key_r, key_c, *refs):
    pieces = refs[: 1 if masks is None else 2]
    x_out, h_out, qkv_out, p_out, o_out, a_out, w = refs[len(pieces) :]
    width = x.shape[2]
    head_tp = heads * HD

    @pl.when(pl.program_id(0) == 0)
    def _():
        place_weights(meta, pieces, masks, w)

    def modulation(i):
        return dot(hot[0], mst[:, i * width : (i + 1) * width], 1, 0)

    xin = x[0].astype(F32)
    normed = norm_rows(xin)[0]
    h = (normed * (1.0 + modulation(1)) + modulation(0)).astype(BF)
    h_out[0] = h
    bias = jnp.where(key_r[...] == key_c[...], 0.0, -1e30) if masked else None
    total = None
    for t in range(w.shape[0]):
        proj = dot(h, w[t, :, : 3 * head_tp], 1, 0).astype(BF)
        qkv_out[0, t] = proj
        outs = []
        for j in range(heads):
            q, k, v = (
                proj[:, i * head_tp + j * HD : i * head_tp + (j + 1) * HD] for i in range(3)
            )
            scores = dot(k, q * jnp.asarray(0.125, BF), 1, 1)
            if masked:
                scores = scores + bias
            e = jnp.exp(scores - jnp.max(scores, axis=0, keepdims=True))
            p = (e * (1.0 / jnp.sum(e, axis=0, keepdims=True))).astype(BF)
            p_out[0, t * heads + j] = p
            outs.append(dot(v, p, 0, 0))
        o = jnp.concatenate(outs, axis=0).T.astype(BF)
        o_out[0, t] = o
        part = dot(o, w[t, :, 3 * head_tp :], 1, 1)
        total = part if total is None else total + part
    a_out[0] = total.astype(BF)
    x_out[0] = (xin + modulation(2) * total).astype(x_out.dtype)


def weight_specs(pieces):
    return [whole(p.shape) for p in pieces]


def forward(meta, x, groups, hot, mst, keys, pieces, masks, n_tp, heads, out_dtype):
    rows, width = x.shape[1], x.shape[2]
    lanes = 4 * heads * HD
    same = hot.shape[0] == 1
    masked = keys is not None
    if keys is None:
        keys = jnp.zeros((rows, 1), jnp.int32), jnp.zeros((1, rows), jnp.int32)

    def out(*shape, dtype=BF):
        zeros = (0,) * (len(shape))
        return (
            jax.ShapeDtypeStruct((groups,) + shape, dtype),
            pl.BlockSpec((1,) + shape, lambda g, meta: (g,) + zeros),
        )

    outs = [
        out(rows, width, dtype=out_dtype),
        out(rows, width),
        out(n_tp, rows, 3 * heads * HD),
        out(n_tp * heads, rows, rows),
        out(n_tp, rows, heads * HD),
        out(rows, width),
    ]
    flops = 2 * groups * rows * width * n_tp * lanes + 4 * groups * rows * rows * n_tp * heads * HD
    return pl.pallas_call(
        functools.partial(forward_kernel, masks, heads, masked),
        out_shape=[o[0] for o in outs],
        grid_spec=pltpu.PrefetchScalarGridSpec(
            num_scalar_prefetch=1,
            grid=(groups,),
            in_specs=[
                pl.BlockSpec((1, rows, width), lambda g, meta: (g + meta[0], 0, 0)),
                pl.BlockSpec(
                    (1, rows, hot.shape[2]), lambda g, meta: (0 if same else g, 0, 0)
                ),
                whole(mst.shape),
                whole(keys[0].shape),
                whole(keys[1].shape),
            ]
            + weight_specs(pieces),
            out_specs=[o[1] for o in outs],
            scratch_shapes=[pltpu.VMEM((n_tp, width, lanes), BF)],
        ),
        compiler_params=params(),
        cost_estimate=pl.CostEstimate(
            flops=flops, bytes_accessed=16 * 2**20, transcendentals=groups * 12 * rows * rows
        ),
    )(meta, x, hot, mst, *keys, *pieces)


def backward_kernel(masks, heads, meta, dx, x, hot, hot_t, mst, a, qkv, p, *refs):
    pieces = refs[: 1 if masks is None else 2]
    dx_out, dqkv_out, da_out, dm_out, w = refs[len(pieces) :]
    width = x.shape[2]
    head_tp = heads * HD
    step = pl.program_id(0)

    @pl.when(step == 0)
    def _():
        place_weights(meta, pieces, masks, w)

    def modulation(i):
        return dot(hot[0], mst[:, i * width : (i + 1) * width], 1, 0)

    grad = dx[0].astype(F32)
    da = (modulation(2) * grad).astype(BF)
    da_out[0] = da
    dh = None
    for t in range(w.shape[0]):
        do = dot(da, w[t, :, 3 * head_tp :], 1, 0).astype(BF)
        got = [[], [], []]
        for j in range(heads):
            q, k, v = (
                qkv[0, t, :, i * head_tp + j * HD : i * head_tp + (j + 1) * HD]
                for i in range(3)
            )
            dop = do[:, j * HD : (j + 1) * HD]
            prob = p[0, t * heads + j]
            dp = dot(v, dop, 1, 1)
            prob32 = prob.astype(F32)
            prod = prob32 * dp
            ds = (prod - prob32 * jnp.sum(prod, axis=0, keepdims=True)).astype(BF)
            got[0].append(dot(k, ds, 0, 0))
            got[1].append(dot(ds, q, 1, 0))
            got[2].append(dot(prob, dop, 1, 0))
        dq = jnp.concatenate(got[0], axis=0).T * 0.125
        dk = jnp.concatenate(got[1], axis=1) * 0.125
        dqkv = jnp.concatenate([dq, dk] + got[2], axis=1).astype(BF)
        dqkv_out[0, t] = dqkv
        part = dot(dqkv, w[t, :, : 3 * head_tp], 1, 1)
        dh = part if dh is None else dh + part
    normed, inverse = norm_rows(x[0].astype(F32))
    dx_out[0] = (grad + norm_back(dh * (1.0 + modulation(1)), normed, inverse)).astype(BF)

    def clip_sum(value):
        return dot(hot_t[0], value.astype(BF), 1, 0)

    sums = [clip_sum(dh), clip_sum(dh * normed), clip_sum(grad * a[0].astype(F32))]

    @pl.when(step == 0)
    def _():
        for i in range(3):
            dm_out[:, i * width : (i + 1) * width] = sums[i]

    @pl.when(step > 0)
    def _():
        for i in range(3):
            dm_out[:, i * width : (i + 1) * width] += sums[i]


def backward(meta, dx, x, hot, hot_t, mst, a, qkv, p, pieces, masks, heads):
    groups, rows, width = dx.shape
    n_tp = qkv.shape[1]
    lanes = 4 * heads * HD
    same = hot.shape[0] == 1
    clips = hot_t.shape[1]

    def blocked(shape, offset=False, fixed=False):
        zeros = (0,) * (len(shape) - 1)
        return pl.BlockSpec(
            (1,) + shape[1:],
            lambda g, meta: (0 if fixed else g + meta[0] if offset else g,) + zeros,
        )

    flops = 2 * groups * rows * width * n_tp * lanes + 8 * groups * rows * rows * n_tp * heads * HD
    return pl.pallas_call(
        functools.partial(backward_kernel, masks, heads),
        out_shape=[
            jax.ShapeDtypeStruct((groups, rows, width), BF),
            jax.ShapeDtypeStruct(qkv.shape, BF),
            jax.ShapeDtypeStruct((groups, rows, width), BF),
            jax.ShapeDtypeStruct((clips, 3 * width), F32),
        ],
        grid_spec=pltpu.PrefetchScalarGridSpec(
            num_scalar_prefetch=1,
            grid=(groups,),
            in_specs=[
                blocked(dx.shape),
                blocked(x.shape, offset=True),
                blocked(hot.shape, fixed=same),
                blocked(hot_t.shape, fixed=same),
                whole(mst.shape),
                blocked(a.shape),
                blocked(qkv.shape),
                blocked(p.shape),
            ]
            + weight_specs(pieces),
            out_specs=[
                blocked((groups, rows, width)),
                blocked(qkv.shape),
                blocked((groups, rows, width)),
                pl.BlockSpec((clips, 3 * width), lambda g, meta: (0, 0)),
            ],
            scratch_shapes=[pltpu.VMEM((n_tp, width, lanes), BF)],
        ),
        compiler_params=params(),
        cost_estimate=pl.CostEstimate(
            flops=flops, bytes_accessed=16 * 2**20, transcendentals=0
        ),
    )(meta, dx, x, hot, hot_t, mst, a, qkv, p, *pieces)


def grads_kernel(masks, row_sp, meta, h, dqkv, da, o, *refs):
    outs, scratch = refs[:-1], refs[-1]
    groups = h.shape[0]
    wide = dqkv.shape[3]
    first, second = None, None
    for g in range(groups):
        one = dot(h[g], dqkv[g, 0], 0, 0)
        two = dot(da[g], o[g, 0], 0, 0)
        first = one if first is None else first + one
        second = two if second is None else second + two
    if masks is None:
        outs[0][0, :, :wide] = first.astype(BF)
        outs[0][0, :, wide:] = second.astype(BF)
        return
    scratch[:, :wide] = first
    scratch[:, wide:] = second
    for place in range(outs[0].shape[1]):
        at = pl.multiple_of((meta[2] ^ masks[place][1]) * row_sp, row_sp)
        outs[0][0, place] = scratch[pl.ds(at, row_sp), :].astype(BF)


def weight_grads(meta, h, dqkv, da, o, masks, row_sp):
    groups, rows, width = h.shape
    n_tp, wide, narrow = dqkv.shape[1], dqkv.shape[3], o.shape[3]
    lanes = wide + narrow
    if masks is None:
        flips = list(range(n_tp))
        shape = (n_tp, width, lanes)
        index = lambda g, meta: (g, 0, 0)
    else:
        flips = [masks[i * (len(masks) // n_tp)][0] for i in range(n_tp)]
        shape = (n_tp, len(masks) // n_tp, row_sp, lanes)
        index = lambda g, meta: (g, 0, 0, 0)

    def tp_of(g, meta):
        if masks is None:
            return g
        flip = 0
        for i, value in enumerate(flips):
            flip = jnp.where(g == i, value, flip)
        return meta[1] ^ flip

    return pl.pallas_call(
        functools.partial(grads_kernel, masks, row_sp),
        out_shape=[jax.ShapeDtypeStruct(shape, BF)],
        grid_spec=pltpu.PrefetchScalarGridSpec(
            num_scalar_prefetch=1,
            grid=(n_tp,),
            in_specs=[
                whole(h.shape),
                pl.BlockSpec((groups, 1, rows, wide), lambda g, m: (0, tp_of(g, m), 0, 0)),
                whole(da.shape),
                pl.BlockSpec((groups, 1, rows, narrow), lambda g, m: (0, tp_of(g, m), 0, 0)),
            ],
            out_specs=[pl.BlockSpec((1,) + shape[1:], index)],
            scratch_shapes=[pltpu.VMEM((width, lanes), F32)],
        ),
        compiler_params=params(),
        cost_estimate=pl.CostEstimate(
            flops=2 * groups * rows * width * n_tp * lanes,
            bytes_accessed=8 * 2**20,
            transcendentals=0,
        ),
    )(meta, h, dqkv, da, o)[0]


GELU_A = 0.7978845608028654
GELU_B = 0.044715


def feed_kernel(
    meta, x2, dy, hot, hot_t, mst, up, down, out, dx_out, dm_out, gup, gdown, h3, da3, acc, dh
):
    width = x2.shape[1]
    step = pl.program_id(0)

    def modulation(i):
        return dot(hot[...], mst[:, i * width : (i + 1) * width], 1, 0)

    @pl.when(step == 0)
    def _():
        normed = norm_rows(x2[...])[0]
        h3[...] = (normed * (1.0 + modulation(1)) + modulation(0)).astype(BF)
        da3[...] = (modulation(2) * dy[...].astype(F32)).astype(BF)
        acc[...] = jnp.zeros_like(acc)
        dh[...] = jnp.zeros_like(dh)

    wu = up[...].reshape(width, -1)
    wd = down[...].reshape(width, -1)
    u = dot(h3[...], wu, 1, 0)
    square = u * u
    th = jnp.tanh(GELU_A * (u + GELU_B * (square * u)))
    g = (0.5 * u * (1.0 + th)).astype(BF)
    slope = 0.5 * (1.0 + th) + (0.5 * GELU_A) * u * (1.0 - th * th) * (
        1.0 + (3.0 * GELU_B) * square
    )
    dg = dot(da3[...], wd, 1, 0)
    du = (dg * slope).astype(BF)
    acc[...] += dot(g, wd, 1, 1)
    dh[...] += dot(du, wu, 1, 1)
    gup[...] = dot(h3[...], du, 0, 0).astype(BF).reshape(gup.shape)
    gdown[...] = dot(da3[...], g, 0, 0).astype(BF).reshape(gdown.shape)

    @pl.when(step == pl.num_programs(0) - 1)
    def _():
        grad = dy[...].astype(F32)
        a3 = acc[...]
        xin = x2[...]
        normed, inverse = norm_rows(xin)
        out[...] = (xin + modulation(2) * a3).astype(BF)
        dh3 = dh[...]
        dx_out[...] = grad + norm_back(dh3 * (1.0 + modulation(1)), normed, inverse)
        for i, value in enumerate([dh3, dh3 * normed, grad * a3]):
            dm_out[:, i * width : (i + 1) * width] = dot(hot_t[...], value.astype(BF), 1, 0)


def feed_forward(meta, x2, dy, hot, hot_t, mst, feed):
    rows, width = x2.shape
    n_tp, n_sp, unused, row_sp, units = feed.shape
    clips = hot_t.shape[0]
    if row_sp % 16:
        blocked = feed.transpose(2, 0, 1, 3, 4).reshape(2, n_tp, width, units)
        up, down = blocked[0], blocked[1]
        specs = [pl.BlockSpec((1, width, units), lambda g, meta: (g, 0, 0))] * 2
        shape = (n_tp, width, units)
    else:
        up = down = feed
        specs = [
            pl.BlockSpec((1, n_sp, 1, row_sp, units), lambda g, meta, i=i: (g, 0, i, 0, 0))
            for i in range(2)
        ]
        shape = (n_tp, n_sp, 1, row_sp, units)
    zeros = (0,) * (len(shape) - 1)
    grad_spec = pl.BlockSpec((1,) + shape[1:], lambda g, meta: (g,) + zeros)
    plain = lambda s: pl.BlockSpec(s, lambda g, meta: (0, 0))
    block_out, dx2, dm, gup, gdown = pl.pallas_call(
        feed_kernel,
        out_shape=[
            jax.ShapeDtypeStruct((rows, width), BF),
            jax.ShapeDtypeStruct((rows, width), F32),
            jax.ShapeDtypeStruct((clips, 3 * width), F32),
            jax.ShapeDtypeStruct(shape, BF),
            jax.ShapeDtypeStruct(shape, BF),
        ],
        grid_spec=pltpu.PrefetchScalarGridSpec(
            num_scalar_prefetch=1,
            grid=(n_tp,),
            in_specs=[
                whole(x2.shape),
                whole(dy.shape),
                whole(hot.shape),
                whole(hot_t.shape),
                whole(mst.shape),
            ]
            + specs,
            out_specs=[
                plain((rows, width)),
                plain((rows, width)),
                plain((clips, 3 * width)),
                grad_spec,
                grad_spec,
            ],
            scratch_shapes=[
                pltpu.VMEM((rows, width), BF),
                pltpu.VMEM((rows, width), BF),
                pltpu.VMEM((rows, width), F32),
                pltpu.VMEM((rows, width), F32),
            ],
        ),
        compiler_params=params(),
        cost_estimate=pl.CostEstimate(
            flops=12 * rows * width * units * n_tp,
            bytes_accessed=40 * 2**20,
            transcendentals=rows * units * n_tp,
        ),
    )(meta, x2, dy, hot, hot_t, mst, up, down)
    both = jnp.concatenate(
        [v.reshape(n_tp, n_sp, 1, row_sp, units) for v in (gup, gdown)], axis=2
    )
    return block_out, dx2, dm, both


def shards(
    tokens, condition, clip_ids, w_mod, w_qkv_s, w_o_s, w_qkv_t, w_o_t, w_up, w_down, grad_out
):
    n_tp, n_sp = lax.axis_size("tp"), lax.axis_size("sp")
    devices = n_tp * n_sp
    my_tp, my_sp = lax.axis_index("tp"), lax.axis_index("sp")
    width = tokens.shape[1]
    sp_frames = tokens.shape[0] // PATCHES
    frames = sp_frames // n_tp
    all_frames = sp_frames * n_sp
    places = PATCHES // devices
    per_block = max(1, min(places, BLOCK_ROWS // all_frames))
    blocks = places // per_block
    rows = all_frames * per_block
    clips = condition.shape[0]
    head_tp = w_o_s.shape[0]
    heads = head_tp // HD
    row_sp = w_up.shape[0]

    sp_bits = bits_of(n_sp)
    tp_bits = bits_of(n_tp)
    far_sp = [("sp", b) for b in reversed(range(1, sp_bits))]
    dims_s = far_sp + [("sp", 0), ("tp", 1), ("tp", 0)]
    dims_t = far_sp + [("tp", 1), ("sp", 0), ("tp", 0)]
    every = [("tp", b) for b in range(tp_bits)] + [("sp", b) for b in range(sp_bits)]
    near = row_sp % 16 == 0

    def gather(w_qkv, w_o, dims):
        flat = w_qkv.transpose(1, 0, 2).reshape(row_sp, -1)
        packed = jnp.concatenate([flat, w_o.T], axis=1)
        if near:
            return near_gather(packed, dims), dims_masks(dims)
        full = in_device_order(cube_gather(packed, dims), dims)
        return [full.reshape(n_tp, width, 4 * head_tp)], None

    def scatter(h, dqkv, da, o):
        if near:
            terms = weight_grads(meta0, h, dqkv, da, o, dims_masks(dims_s), row_sp)
            terms = terms.reshape(2, devices // 2, row_sp, 4 * head_tp)
            mine = near_scatter(terms[0], terms[1], dims_s)
        else:
            terms = weight_grads(meta0, h, dqkv, da, o, None, row_sp)
            terms = terms.reshape(devices, row_sp, 4 * head_tp)
            mine = cube_scatter(in_device_order(terms, dims_s, back=True), dims_s)
        mine = mine.reshape(row_sp, 4, head_tp)
        return mine[:, :3].transpose(1, 0, 2), mine[:, 3].T

    feed = lax.all_gather(jnp.stack([w_up, w_down.T]), ("tp", "sp"), axis=0)
    feed = feed.reshape(n_tp, n_sp, 2, row_sp, -1)

    cond_act = jax.nn.silu(condition).astype(BF)
    cond_rows = lax.dynamic_slice_in_dim(cond_act, my_sp * row_sp, row_sp, axis=1)
    modulation = cube_sum(
        jnp.dot(cond_rows, w_mod, preferred_element_type=F32),
        [("sp", b) for b in range(sp_bits)],
    )
    pieces_s, masks_s = gather(w_qkv_s, w_o_s, dims_s)
    pieces_t, masks_t = gather(w_qkv_t, w_o_t, dims_t)
    coarse = lax.reduce_precision(modulation, 8, 7)
    mst = jnp.concatenate([coarse, modulation - coarse]).astype(BF)
    mst_s, mst_t, mst_f = (
        mst[:, i * 3 * width : (i + 1) * 3 * width] for i in range(3)
    )

    def hot_of(ids):
        hot = (ids[..., None] == jnp.arange(clips, dtype=jnp.int32)).astype(BF)
        return jnp.concatenate([hot, hot], axis=-1), jnp.swapaxes(hot, -1, -2)

    first = my_sp * sp_frames + my_tp * frames
    ids_s = lax.dynamic_slice_in_dim(clip_ids, first, frames)
    hot_s, hot_s_t = hot_of(jnp.repeat(ids_s[:, None], PATCHES, axis=1))
    ids_t = jnp.repeat(clip_ids, per_block)
    hot_t, hot_t_t = hot_of(ids_t[None])
    hot_f, hot_f_t = hot_of(jnp.tile(ids_t, blocks))
    key = ids_t * per_block + jnp.tile(jnp.arange(per_block, dtype=jnp.int32), all_frames)
    keys = key[:, None], key[None, :]
    meta0 = jnp.stack([0 * my_tp, my_tp, my_sp]).astype(jnp.int32)
    meta_s = jnp.stack([my_tp * frames, my_tp, my_sp]).astype(jnp.int32)

    def to_places(value):
        split = value.reshape(frames, devices, blocks, per_block, width).transpose(1, 2, 0, 3, 4)
        got = lax.all_to_all(split, ("sp", "tp"), 0, 0, tiled=True)
        return got.transpose(1, 0, 2, 3, 4).reshape(blocks, rows, width)

    def to_frames(value):
        split = value.reshape(blocks, devices, frames, per_block, width).transpose(1, 0, 2, 3, 4)
        got = lax.all_to_all(split, ("sp", "tp"), 0, 0, tiled=True)
        return got.transpose(2, 0, 1, 3, 4).reshape(frames, PATCHES, width)

    def input_to_places(value):
        split = value.reshape(sp_frames, n_sp, n_tp, blocks, per_block, width)
        split = lax.dynamic_slice_in_dim(split, my_tp, 1, axis=2)[:, :, 0]
        got = lax.all_to_all(split.transpose(1, 2, 0, 3, 4), "sp", 0, 0, tiled=True)
        return got.transpose(1, 0, 2, 3, 4).reshape(blocks * rows, width)

    def places_to_output(value):
        split = value.reshape(blocks, n_sp, sp_frames, per_block, width).transpose(1, 0, 2, 3, 4)
        got = lax.all_to_all(split, "sp", 0, 0, tiled=True)
        got = lax.all_gather(got, "tp", axis=0)
        return got.transpose(3, 1, 0, 2, 4, 5).reshape(-1, width)

    grad_rows = input_to_places(grad_out)

    own = tokens.reshape(sp_frames, PATCHES, width)
    x1_frames, h1, qkv1, p1, o1, a1 = forward(
        meta_s, own, frames, hot_s, mst_s, None, pieces_s, masks_s, n_tp, heads, BF
    )
    x1 = to_places(x1_frames)
    x2, h2, qkv2, p2, o2, a2 = forward(
        meta0, x1, blocks, hot_t, mst_t, keys, pieces_t, masks_t, n_tp, heads, F32
    )

    block_out, dx2, dm_f, feed_grad = feed_forward(
        meta0, x2.reshape(blocks * rows, width), grad_rows, hot_f, hot_f_t, mst_f, feed
    )
    feed_grad = lax.psum_scatter(
        feed_grad.reshape(devices, 2, row_sp, -1), ("tp", "sp"), scatter_dimension=0
    ).astype(F32)

    dx1, dqkv2, da2, dm_t = backward(
        meta0, dx2.reshape(blocks, rows, width), x1, hot_t, hot_t_t, mst_t, a2, qkv2, p2,
        pieces_t, masks_t, heads,
    )
    dx1_frames = to_frames(dx1)
    sum_qt, sum_ot = scatter(h2, dqkv2, da2, o2)
    block_out = places_to_output(block_out)

    dx0, dqkv1, da1, dm_s = backward(
        meta_s, dx1_frames, own, hot_s, hot_s_t, mst_s, a1, qkv1, p1, pieces_s, masks_s, heads
    )
    sum_qs, sum_os = scatter(h1, dqkv1, da1, o1)
    grad_tokens = lax.all_gather(dx0.reshape(-1, width), "tp", axis=0, tiled=True)

    dm_rest = cube_sum(jnp.concatenate([dm_t, dm_f], axis=-1), every)
    dm_s = cube_sum(dm_s, every)
    dm_low = jnp.concatenate([dm_s, dm_rest], axis=-1).astype(BF)
    grad_mod = jnp.dot(cond_rows.T, dm_low, preferred_element_type=F32)
    grad_act = jnp.dot(dm_low, w_mod.T, preferred_element_type=F32)
    sp_dims = [("sp", b) for b in range(sp_bits)]
    grad_act = cube_gather(grad_act, sp_dims).transpose(1, 0, 2).reshape(clips, width)
    unused, silu_pull = jax.vjp(jax.nn.silu, condition)
    grad_condition = silu_pull(grad_act)[0]
    return (
        block_out,
        grad_tokens,
        grad_condition,
        grad_mod,
        sum_qs,
        sum_os,
        sum_qt,
        sum_ot,
        feed_grad[0],
        feed_grad[1].T,
    )


def solution(mesh):
    placed = (
        P("sp", None),
        P(),
        P(),
        P("sp", None),
        P(None, "sp", "tp"),
        P("tp", "sp"),
        P(None, "sp", "tp"),
        P("tp", "sp"),
        P("sp", "tp"),
        P("tp", "sp"),
        P("sp", None),
    )
    return jax.shard_map(
        shards,
        mesh=mesh,
        in_specs=placed,
        out_specs=(
            P("sp", None),
            P("sp", None),
            P(),
            P("sp", None),
            P(None, "sp", "tp"),
            P("tp", "sp"),
            P(None, "sp", "tp"),
            P("tp", "sp"),
            P("sp", "tp"),
            P("tp", "sp"),
        ),
        check_vma=False,
    )
```

```python
import functools

import jax
import jax.numpy as jnp
from jax import lax
from jax.experimental import pallas as pl
from jax.experimental.pallas import tpu as pltpu
from jax.sharding import PartitionSpec as P

HD = 64
PATCHES = 256
BLOCK_ROWS = 256
FEED_STEP = 2
TOKENS_STEP = 3
COSTS = (20, 20, 20, 1)
EPSILON = 1e-06
HIGHEST = lax.Precision.HIGHEST
BF = jnp.bfloat16
F32 = jnp.float32


def bits_of(size):
    return size.bit_length() - 1


def swap(value, axis, bit):
    size = lax.axis_size(axis)
    return lax.ppermute(value, axis, [(i, i ^ (1 << bit)) for i in range(size)])


def my_bit(axis, bit):
    return (lax.axis_index(axis) >> bit) & 1


def cube_sum(value, dims):
    for axis, bit in dims:
        value = value + swap(value, axis, bit)
    return value


def cube_gather(block, dims):
    held = block[None]
    for axis, bit in dims:
        other = swap(held, axis, bit)
        high = my_bit(axis, bit) == 1
        held = jnp.concatenate([jnp.where(high, other, held), jnp.where(high, held, other)])
    return held


def cube_scatter(parts, dims):
    for axis, bit in reversed(dims):
        half = parts.shape[0] // 2
        mine = my_bit(axis, bit)
        send = lax.dynamic_slice_in_dim(parts, (1 - mine) * half, half)
        keep = lax.dynamic_slice_in_dim(parts, mine * half, half)
        got = swap(send, axis, bit)
        parts = keep.astype(F32) + got.astype(F32)
        if half > 1:
            parts = parts.astype(BF)
    return parts[0]


def in_device_order(gathered, dims, back=False):
    count = len(dims)
    want = [("tp", b) for b in reversed(range(bits_of(lax.axis_size("tp"))))]
    want += [("sp", b) for b in reversed(range(bits_of(lax.axis_size("sp"))))]
    have = list(reversed(dims))
    tail = gathered.shape[1:]
    if back:
        have, want = want, have
    split = gathered.reshape((2,) * count + tail)
    order = [have.index(w) for w in want]
    split = split.transpose(order + [count + i for i in range(len(tail))])
    return split.reshape((2**count,) + tail)


VMEM_BYTES = 52 * 1024 * 1024


def cost(micros):
    return pl.CostEstimate(flops=micros * 10**9, bytes_accessed=2**10, transcendentals=0)


def after(value, *others):
    return lax.optimization_barrier((value,) + others)[0]


class Chain:
    def __init__(self, state, steps):
        self.state, self.steps = tuple(state), list(steps)

    def go(self):
        if self.steps:
            self.state = tuple(self.steps.pop(0)(*self.state))

    def run(self):
        while self.steps:
            self.go()
        return self.state


def stage(chains, *values):
    states, values = lax.optimization_barrier(([c.state for c in chains], values))
    for chain, state in zip(chains, states):
        chain.state = tuple(state)
    return values if len(values) != 1 else values[0]


def gather_chain(block, far, last):
    def far_step(dim):
        return lambda held: (jnp.concatenate([held, swap(held, *dim)]),)

    def split(held):
        half = held.shape[1] // 2
        one, two = held[:, :half], held[:, half:]
        return (
            jnp.concatenate([one, swap(one, *last[0])]),
            jnp.concatenate([two, swap(two, *last[1])]),
        )

    def join(one, two):
        return (jnp.concatenate([one, swap(one, *last[1]), two, swap(two, *last[0])]),)

    def final(held):
        return (held, swap(held, *last[2]))

    return Chain((block[None],), [far_step(d) for d in far] + [split, join, final])


def scatter_chain(mine, other, far, last):
    def add(left, right):
        return left.astype(F32) + right.astype(F32)

    def first(mine, other):
        total = add(mine, swap(other, *last[2]))
        count, rows = total.shape[0], total.shape[1]
        total = total.reshape((2, 2, count // 4, 2, rows // 2) + total.shape[2:]).astype(BF)
        one, two = total[:, :, :, 0], total[:, :, :, 1]
        return one[0], one[1], two[:, 0], two[:, 1]

    def second(keep_one, send_one, keep_two, send_two):
        one = add(keep_one, swap(send_one, *last[1])).astype(BF)
        two = add(keep_two, swap(send_two, *last[0])).astype(BF)
        return one[0], one[1], two[0], two[1]

    def third(keep_one, send_one, keep_two, send_two):
        one = add(keep_one, swap(send_one, *last[0])).astype(BF)
        two = add(keep_two, swap(send_two, *last[1])).astype(BF)
        both = jnp.concatenate([one, two], axis=1)
        half = both.shape[0] // 2
        return both[:half], both[half:]

    def far_step(dim):
        def step(keep, send):
            total = add(keep, swap(send, *dim))
            half = total.shape[0] // 2
            if half == 0:
                return (total[0],)
            total = total.astype(BF)
            return total[:half], total[half:]

        return step

    return Chain((mine, other), [first, second, third] + [far_step(d) for d in reversed(far)])


def sum_chain(value, dims):
    def step(axis, bits):
        masks = [0]
        for bit in bits:
            masks += [m | 1 << bit for m in masks]
        size = lax.axis_size(axis)

        def run(value):
            others = [lax.ppermute(value, axis, [(i, i ^ m) for i in range(size)]) for m in masks[1:]]
            return (sum(others, value),)

        return run

    return Chain((value,), [step(*d) for d in dims])


def dims_masks(dims):
    masks = []
    for m in range(2 ** len(dims)):
        flip = {"tp": 0, "sp": 0}
        for place, (axis, bit) in enumerate(dims):
            flip[axis] |= ((m >> place) & 1) << bit
        masks.append((flip["tp"], flip["sp"]))
    return masks


def piece_masks(far, last):
    masks = []
    for core in range(2):
        for half in range(2):
            pair = last[:2] if half == 0 else last[1::-1]
            for tp_flip, sp_flip in dims_masks(far + pair):
                masks.append((tp_flip | core << last[2][1], sp_flip, half))
    return masks


def dot(left, right, left_dim, right_dim):
    return lax.dot_general(
        left, right, (((left_dim,), (right_dim,)), ((), ())), preferred_element_type=F32
    )


def norm_rows(operand):
    centred = operand - jnp.mean(operand, axis=-1, keepdims=True)
    inverse = lax.rsqrt(jnp.mean(centred * centred, axis=-1, keepdims=True) + EPSILON)
    return (centred * inverse, inverse)


def norm_back(incoming, normed, inverse):
    first_mean = jnp.mean(incoming, axis=-1, keepdims=True)
    second_mean = jnp.mean(incoming * normed, axis=-1, keepdims=True)
    return inverse * (incoming - first_mean - normed * second_mean)


def params(count=1):
    return pltpu.CompilerParams(
        dimension_semantics=("arbitrary",) * count, vmem_limit_bytes=VMEM_BYTES
    )


def whole(shape):
    zeros = (0,) * len(shape)
    return pl.BlockSpec(shape, lambda g, meta: zeros, pipeline_mode=pl.Buffered(1))


def place_weights(meta, pieces, masks, target):
    if masks is None:
        target[...] = pieces[0][...].reshape(target.shape)
        return
    rows = pieces[0].shape[1]
    count = pieces[0].shape[0]
    for m, (tp_flip, sp_flip, half) in enumerate(masks):
        at = pl.multiple_of((meta[2] ^ sp_flip) * (2 * rows) + half * rows, rows)
        target[meta[1] ^ tp_flip, pl.ds(at, rows), :] = pieces[m // count][m % count]


def split_places(pair):
    count, width = pair.shape[0], pair.shape[3]
    one, two = pair[:, 0], pair[:, 1]
    upper = lax.broadcasted_iota(jnp.int32, one.shape, 1) < 4
    left = jnp.where(upper, one, pltpu.roll(two, 4, 1))
    right = jnp.where(upper, pltpu.roll(one, 4, 1), two)
    return left.reshape(count * 8, width), right.reshape(count * 8, width)


def join_places(left, right):
    count, width = left.shape[0] // 8, left.shape[1]
    left, right = left.reshape(count, 8, width), right.reshape(count, 8, width)
    upper = lax.broadcasted_iota(jnp.int32, left.shape, 1) < 4
    one = jnp.where(upper, left, pltpu.roll(right, 4, 1))
    two = jnp.where(upper, pltpu.roll(left, 4, 1), right)
    return one, two


def forward_kernel(masks, heads, masked, meta, x, hot, mst, key_r, key_c, *refs):
    pieces = refs[: 1 if masks is None else 2]
    x_out, h_out, qkv_out, p_out, o_out, a_out, w, both = refs[len(pieces) :]
    width = x.shape[-1]
    head_tp = heads * HD
    step = pl.program_id(0)
    zipped = len(x.shape) == 4

    @pl.when(step == 0)
    def _():
        place_weights(meta, pieces, masks, w)
        if zipped:
            both[0], both[1] = split_places(x[...].astype(F32))

    def modulation(i):
        return dot(hot[0], mst[:, i * width : (i + 1) * width], 1, 0)

    xin = both[step] if zipped else x[0].astype(F32)
    normed = norm_rows(xin)[0]
    h = (normed * (1.0 + modulation(1)) + modulation(0)).astype(BF)
    h_out[0] = h
    bias = jnp.where(key_r[...] == key_c[...], 0.0, -1e30) if masked else None
    total = None
    for t in range(w.shape[0]):
        proj = dot(h, w[t, :, : 3 * head_tp], 1, 0).astype(BF)
        qkv_out[0, t] = proj
        outs = []
        for j in range(heads):
            q, k, v = (
                proj[:, i * head_tp + j * HD : i * head_tp + (j + 1) * HD] for i in range(3)
            )
            scores = dot(k, q * jnp.asarray(0.125, BF), 1, 1)
            if masked:
                scores = scores + bias
            e = jnp.exp(scores - jnp.max(scores, axis=0, keepdims=True))
            p = (e * (1.0 / jnp.sum(e, axis=0, keepdims=True))).astype(BF)
            p_out[0, t * heads + j] = p
            outs.append(dot(v, p, 0, 0))
        o = jnp.concatenate(outs, axis=0).T.astype(BF)
        o_out[0, t] = o
        part = dot(o, w[t, :, 3 * head_tp :], 1, 1)
        total = part if total is None else total + part
    a_out[0] = total.astype(BF)
    x_new = xin + modulation(2) * total
    if zipped:
        both[step] = x_new

        @pl.when(step == 1)
        def _():
            one, two = join_places(both[0], both[1])
            x_out[:, 0], x_out[:, 1] = one.astype(x_out.dtype), two.astype(x_out.dtype)
    else:
        x_out[...] = x_new.reshape(x_out.shape).astype(x_out.dtype)


def weight_specs(pieces):
    return [whole(p.shape) for p in pieces]


def forward(meta, x, groups, rows, hot, mst, keys, pieces, masks, n_tp, heads, x_shape, out_dtype):
    width = x.shape[-1]
    lanes = 4 * heads * HD
    same = hot.shape[0] == 1
    masked = keys is not None
    zipped = x.ndim == 4
    if keys is None:
        keys = jnp.zeros((rows, 1), jnp.int32), jnp.zeros((1, rows), jnp.int32)

    def out(*shape):
        zeros = (0,) * len(shape)
        return (
            jax.ShapeDtypeStruct((groups,) + shape, BF),
            pl.BlockSpec((1,) + shape, lambda g, meta: (g,) + zeros),
        )

    if zipped:
        x_spec = whole(x.shape)
        x_out = whole(x_shape)
    else:
        x_spec = pl.BlockSpec((1, rows, width), lambda g, meta: (g + meta[0], 0, 0))
        if len(x_shape) == 4:
            x_out = pl.BlockSpec(
                (x_shape[0], 1) + x_shape[2:], lambda g, meta: (0, g, 0, 0)
            )
        else:
            x_out = pl.BlockSpec((1, rows, width), lambda g, meta: (g, 0, 0))
    outs = [
        (jax.ShapeDtypeStruct(x_shape, out_dtype), x_out),
        out(rows, width),
        out(n_tp, rows, 3 * heads * HD),
        out(n_tp * heads, rows, rows),
        out(n_tp, rows, heads * HD),
        out(rows, width),
    ]
    return pl.pallas_call(
        functools.partial(forward_kernel, masks, heads, masked),
        out_shape=[o[0] for o in outs],
        grid_spec=pltpu.PrefetchScalarGridSpec(
            num_scalar_prefetch=1,
            grid=(groups,),
            in_specs=[
                x_spec,
                pl.BlockSpec(
                    (1, rows, hot.shape[2]), lambda g, meta: (0 if same else g, 0, 0)
                ),
                whole(mst.shape),
                whole(keys[0].shape),
                whole(keys[1].shape),
            ]
            + weight_specs(pieces),
            out_specs=[o[1] for o in outs],
            scratch_shapes=[
                pltpu.VMEM((n_tp, width, lanes), BF),
                pltpu.VMEM((groups, rows, width) if zipped else (1, 8, 128), F32),
            ],
        ),
        compiler_params=params(),
        cost_estimate=cost(COSTS[0]),
    )(meta, x, hot, mst, *keys, *pieces)


def backward_kernel(masks, heads, meta, dx, x, hot, hot_t, mst, a, qkv, p, *refs):
    pieces = refs[: 1 if masks is None else 2]
    dx_out, dqkv_out, da_out, dm_out, w, both, grads = refs[len(pieces) :]
    width = x.shape[-1]
    head_tp = heads * HD
    step = pl.program_id(0)
    zipped = len(x.shape) == 4

    @pl.when(step == 0)
    def _():
        place_weights(meta, pieces, masks, w)
        if zipped:
            both[0], both[1] = split_places(x[...].astype(F32))
            grads[0], grads[1] = split_places(dx[...].astype(F32))

    def modulation(i):
        return dot(hot[0], mst[:, i * width : (i + 1) * width], 1, 0)

    if zipped:
        grad = grads[step]
    else:
        grad = dx[...].astype(F32).reshape(x.shape[1:])
    da = (modulation(2) * grad).astype(BF)
    da_out[0] = da
    dh = None
    for t in range(w.shape[0]):
        do = dot(da, w[t, :, 3 * head_tp :], 1, 0).astype(BF)
        got = [[], [], []]
        for j in range(heads):
            q, k, v = (
                qkv[0, t, :, i * head_tp + j * HD : i * head_tp + (j + 1) * HD]
                for i in range(3)
            )
            dop = do[:, j * HD : (j + 1) * HD]
            prob = p[0, t * heads + j]
            dp = dot(v, dop, 1, 1)
            prob32 = prob.astype(F32)
            prod = prob32 * dp
            ds = (prod - prob32 * jnp.sum(prod, axis=0, keepdims=True)).astype(BF)
            got[0].append(dot(k, ds, 0, 0))
            got[1].append(dot(ds, q, 1, 0))
            got[2].append(dot(prob, dop, 1, 0))
        dq = jnp.concatenate(got[0], axis=0).T * 0.125
        dk = jnp.concatenate(got[1], axis=1) * 0.125
        dqkv = jnp.concatenate([dq, dk] + got[2], axis=1).astype(BF)
        dqkv_out[0, t] = dqkv
        part = dot(dqkv, w[t, :, : 3 * head_tp], 1, 1)
        dh = part if dh is None else dh + part
    normed, inverse = norm_rows(both[step] if zipped else x[0].astype(F32))
    dx_new = grad + norm_back(dh * (1.0 + modulation(1)), normed, inverse)
    if zipped:
        grads[step] = dx_new

        @pl.when(step == 1)
        def _():
            one, two = join_places(grads[0], grads[1])
            dx_out[:, 0], dx_out[:, 1] = one.astype(BF), two.astype(BF)
    else:
        dx_out[0] = dx_new.astype(BF)

    def clip_sum(value):
        return dot(hot_t[0], value.astype(BF), 1, 0)

    sums = [clip_sum(dh), clip_sum(dh * normed), clip_sum(grad * a[0].astype(F32))]

    @pl.when(step == 0)
    def _():
        for i in range(3):
            dm_out[:, i * width : (i + 1) * width] = sums[i]

    @pl.when(step > 0)
    def _():
        for i in range(3):
            dm_out[:, i * width : (i + 1) * width] += sums[i]


def backward(meta, dx, x, hot, hot_t, mst, a, qkv, p, pieces, masks, heads):
    groups, n_tp, rows = qkv.shape[:3]
    width = dx.shape[-1]
    zipped = x.ndim == 4
    lanes = 4 * heads * HD
    same = hot.shape[0] == 1
    clips = hot_t.shape[1]

    def blocked(shape, offset=False, fixed=False):
        zeros = (0,) * (len(shape) - 1)
        return pl.BlockSpec(
            (1,) + shape[1:],
            lambda g, meta: (0 if fixed else g + meta[0] if offset else g,) + zeros,
        )

    if zipped:
        dx_spec, x_spec, dx_out, dx_shape = whole(dx.shape), whole(x.shape), whole(x.shape), x.shape
    else:
        x_spec = blocked(x.shape, offset=True)
        dx_shape = (groups, rows, width)
        dx_out = blocked(dx_shape)
        if dx.ndim == 4:
            dx_spec = pl.BlockSpec((dx.shape[0], 1) + dx.shape[2:], lambda g, meta: (0, g, 0, 0))
        else:
            dx_spec = blocked(dx.shape)
    return pl.pallas_call(
        functools.partial(backward_kernel, masks, heads),
        out_shape=[
            jax.ShapeDtypeStruct(dx_shape, BF),
            jax.ShapeDtypeStruct(qkv.shape, BF),
            jax.ShapeDtypeStruct((groups, rows, width), BF),
            jax.ShapeDtypeStruct((clips, 3 * width), F32),
        ],
        grid_spec=pltpu.PrefetchScalarGridSpec(
            num_scalar_prefetch=1,
            grid=(groups,),
            in_specs=[
                dx_spec,
                x_spec,
                blocked(hot.shape, fixed=same),
                blocked(hot_t.shape, fixed=same),
                whole(mst.shape),
                blocked(a.shape),
                blocked(qkv.shape),
                blocked(p.shape),
            ]
            + weight_specs(pieces),
            out_specs=[
                dx_out,
                blocked(qkv.shape),
                blocked((groups, rows, width)),
                pl.BlockSpec((clips, 3 * width), lambda g, meta: (0, 0)),
            ],
            scratch_shapes=[
                pltpu.VMEM((n_tp, width, lanes), BF),
                pltpu.VMEM((groups, rows, width) if zipped else (1, 8, 128), F32),
                pltpu.VMEM((groups, rows, width) if zipped else (1, 8, 128), F32),
            ],
        ),
        compiler_params=params(),
        cost_estimate=cost(COSTS[1]),
    )(meta, dx, x, hot, hot_t, mst, a, qkv, p, *pieces)


def store_blocks(meta, masks, scratch, target):
    count, rows = target.shape[0], target.shape[1]
    for place in range(count):
        at = pl.multiple_of((meta[2] ^ masks[place][1]) * rows, rows)
        target[place] = scratch[pl.ds(at, rows), :]


def tp_of(masks, n_tp, g, meta):
    if masks is None:
        return g
    flips = [masks[i * (len(masks) // n_tp)][0] for i in range(n_tp)]
    flips = flips[n_tp // 2 :] + flips[: n_tp // 2]
    flip = 0
    for i, value in enumerate(flips):
        flip = jnp.where(g == i, value, flip)
    return meta[1] ^ flip


def grads_kernel(masks, meta, h, dqkv, da, o, *refs):
    outs, scratch = refs[:-1], refs[-1]
    groups = h.shape[0]
    wide = dqkv.shape[3]
    first, second = None, None
    for g in range(groups):
        one = dot(h[g], dqkv[g, 0], 0, 0)
        two = dot(da[g], o[g, 0], 0, 0)
        first = one if first is None else first + one
        second = two if second is None else second + two
    if masks is None:
        outs[0][0, :, :wide] = first.astype(BF)
        outs[0][0, :, wide:] = second.astype(BF)
        return
    scratch[:, :wide] = first.astype(BF)
    scratch[:, wide:] = second.astype(BF)
    step = pl.program_id(0)
    half = pl.num_programs(0) // 2

    @pl.when(step < half)
    def _():
        store_blocks(meta, masks, scratch, outs[0].at[0])

    @pl.when(step >= half)
    def _():
        store_blocks(meta, masks, scratch, outs[1].at[0])


def half_specs(n_tp, shape):
    zeros = (0,) * len(shape)
    half = n_tp // 2
    return [
        pl.BlockSpec((1,) + shape, lambda g, meta: (jnp.minimum(g, half - 1),) + zeros),
        pl.BlockSpec((1,) + shape, lambda g, meta: (jnp.maximum(g - half, 0),) + zeros),
    ]


def weight_grads(meta, h, dqkv, da, o, masks, row_sp):
    groups, rows, width = h.shape
    n_tp, wide, narrow = dqkv.shape[1], dqkv.shape[3], o.shape[3]
    lanes = wide + narrow
    if masks is None:
        out_shape = [jax.ShapeDtypeStruct((n_tp, width, lanes), BF)]
        out_specs = [pl.BlockSpec((1, width, lanes), lambda g, meta: (g, 0, 0))]
    else:
        shape = (len(masks) // n_tp, row_sp, lanes)
        out_shape = [jax.ShapeDtypeStruct((n_tp // 2,) + shape, BF)] * 2
        out_specs = half_specs(n_tp, shape)
    at = lambda g, meta: (0, tp_of(masks, n_tp, g, meta), 0, 0)
    return pl.pallas_call(
        functools.partial(grads_kernel, masks),
        out_shape=out_shape,
        grid_spec=pltpu.PrefetchScalarGridSpec(
            num_scalar_prefetch=1,
            grid=(n_tp,),
            in_specs=[
                whole(h.shape),
                pl.BlockSpec((groups, 1, rows, wide), at),
                whole(da.shape),
                pl.BlockSpec((groups, 1, rows, narrow), at),
            ],
            out_specs=out_specs,
            scratch_shapes=[pltpu.VMEM((width, lanes), BF)],
        ),
        compiler_params=params(),
        cost_estimate=cost(COSTS[2]),
    )(meta, h, dqkv, da, o)


GELU_A = 0.7978845608028654
GELU_B = 0.044715


def feed_kernel(masks, last_call, meta, x2, dy, hot, hot_t, mst, up, down, *refs):
    if last_call:
        acc_in, dh_in, out, dx_out, dm_out, *grads, h3, da3, acc, dh, blocks = refs
    else:
        acc, dh, *grads, h3, da3, blocks = refs
    width = x2.shape[1]
    step = pl.program_id(0)

    def modulation(i):
        return dot(hot[...], mst[:, i * width : (i + 1) * width], 1, 0)

    @pl.when(step == 0)
    def _():
        normed = norm_rows(x2[...])[0]
        h3[...] = (normed * (1.0 + modulation(1)) + modulation(0)).astype(BF)
        da3[...] = (modulation(2) * dy[...].astype(F32)).astype(BF)
        if last_call:
            acc[...], dh[...] = acc_in[...], dh_in[...]
        else:
            acc[...] = jnp.zeros_like(acc)
            dh[...] = jnp.zeros_like(dh)

    wu = up[...].reshape(width, -1)
    wd = down[...].reshape(width, -1)
    u = dot(h3[...], wu, 1, 0)
    square = u * u
    th = jnp.tanh(GELU_A * (u + GELU_B * (square * u)))
    g = (0.5 * u * (1.0 + th)).astype(BF)
    slope = 0.5 * (1.0 + th) + (0.5 * GELU_A) * u * (1.0 - th * th) * (
        1.0 + (3.0 * GELU_B) * square
    )
    dg = dot(da3[...], wd, 1, 0)
    du = (dg * slope).astype(BF)
    acc[...] += dot(g, wd, 1, 1)
    dh[...] += dot(du, wu, 1, 1)
    grad_up = dot(h3[...], du, 0, 0).astype(BF)
    grad_down = dot(da3[...], g, 0, 0).astype(BF)
    if masks is None:
        grads[0][0], grads[1][0] = grad_up, grad_down
    else:
        for i, value in enumerate((grad_up, grad_down)):
            blocks[...] = value
            store_blocks(meta, masks, blocks, grads[0].at[0, :, i])

    if last_call:

        @pl.when(step == pl.num_programs(0) - 1)
        def _():
            grad = dy[...].astype(F32)
            a3 = acc[...]
            xin = x2[...]
            normed, inverse = norm_rows(xin)
            out[...] = (xin + modulation(2) * a3).astype(BF)
            dh3 = dh[...]
            dx_out[...] = grad + norm_back(dh3 * (1.0 + modulation(1)), normed, inverse)
            for i, value in enumerate([dh3, dh3 * normed, grad * a3]):
                dm_out[:, i * width : (i + 1) * width] = dot(hot_t[...], value.astype(BF), 1, 0)


def feed_half(meta, x2, dy, hot, hot_t, mst, weights, masks, sums):
    rows, width = x2.shape
    n_tp, n_sp, unused, row_sp, units = weights.shape
    clips = hot_t.shape[0]
    half = n_tp // 2
    last_call = sums is not None
    start = half if last_call else 0
    at = lambda g, meta: tp_of(masks, n_tp, g + start, meta)
    if masks is None:
        blocked = weights.transpose(2, 0, 1, 3, 4).reshape(2, n_tp, width, units)
        up, down = blocked[0], blocked[1]
        specs = [pl.BlockSpec((1, width, units), lambda g, meta: (g + start, 0, 0))] * 2
        grad_shapes = [(half, width, units)] * 2
    else:
        up = down = weights
        specs = [
            pl.BlockSpec(
                (1, n_sp, 1, row_sp, units), lambda g, meta, i=i: (at(g, meta), 0, i, 0, 0)
            )
            for i in range(2)
        ]
        grad_shapes = [(half, n_sp, 2, row_sp, units)]
    zeros = (0,) * (len(grad_shapes[0]) - 1)
    grad_spec = pl.BlockSpec((1,) + grad_shapes[0][1:], lambda g, meta: (g,) + zeros)
    plain = lambda s: pl.BlockSpec(s, lambda g, meta: (0, 0))
    total = pltpu.VMEM((rows, width), F32)
    kept = [pltpu.VMEM((rows, width), BF), pltpu.VMEM((rows, width), BF)]
    if last_call:
        out_types = [((rows, width), BF), ((rows, width), F32), ((clips, 3 * width), F32)]
        scratch = kept + [total, total]
    else:
        out_types = [((rows, width), F32), ((rows, width), F32)]
        scratch = kept
    return pl.pallas_call(
        functools.partial(feed_kernel, masks, last_call),
        out_shape=[jax.ShapeDtypeStruct(*t) for t in out_types]
        + [jax.ShapeDtypeStruct(g, BF) for g in grad_shapes],
        grid_spec=pltpu.PrefetchScalarGridSpec(
            num_scalar_prefetch=1,
            grid=(half,),
            in_specs=[
                whole(x2.shape),
                whole(dy.shape),
                whole(hot.shape),
                whole(hot_t.shape),
                whole(mst.shape),
            ]
            + specs
            + ([whole(x2.shape)] * 2 if last_call else []),
            out_specs=[plain(t[0]) for t in out_types] + [grad_spec] * len(grad_shapes),
            scratch_shapes=scratch + [pltpu.VMEM((width, units), BF)],
        ),
        compiler_params=params(),
        cost_estimate=cost(COSTS[3]),
    )(meta, x2, dy, hot, hot_t, mst, up, down, *(sums or ()))


def shards(
    tokens, condition, clip_ids, w_mod, w_qkv_s, w_o_s, w_qkv_t, w_o_t, w_up, w_down, grad_out
):
    n_tp, n_sp = lax.axis_size("tp"), lax.axis_size("sp")
    devices = n_tp * n_sp
    my_tp, my_sp = lax.axis_index("tp"), lax.axis_index("sp")
    width = tokens.shape[1]
    sp_frames = tokens.shape[0] // PATCHES
    frames = sp_frames // n_tp
    all_frames = sp_frames * n_sp
    places = PATCHES // devices
    per_block = max(1, min(places, BLOCK_ROWS // all_frames))
    blocks = places // per_block
    rows = all_frames * per_block
    clips = condition.shape[0]
    head_tp = w_o_s.shape[0]
    heads = head_tp // HD
    row_sp = w_up.shape[0]
    zipped = (frames, per_block, blocks) == (2, 4, 2)

    sp_bits = bits_of(n_sp)
    tp_bits = bits_of(n_tp)
    far = [("sp", b) for b in reversed(range(1, sp_bits))]
    last = [("sp", 0), ("tp", 1), ("tp", 0)]
    every = [("tp", b) for b in range(tp_bits)] + [("sp", b) for b in range(sp_bits)]
    sp_dims = [("sp", b) for b in range(sp_bits)]
    near = row_sp % 32 == 0

    def pack(w_qkv, w_o):
        flat = w_qkv.transpose(1, 0, 2).reshape(row_sp, -1)
        return jnp.concatenate([flat, w_o.T], axis=1)

    masks = dims_masks(far + last) if near else None

    def scatter(terms):
        if near:
            other, mine = (v.reshape((devices // 2, -1) + v.shape[-1:]) for v in terms)
            return scatter_chain(mine, other, far, last)
        terms = terms[0].reshape((devices, -1) + terms[0].shape[-1:])
        terms = in_device_order(terms, far + last, back=True)
        return Chain((terms,), [lambda v: (cube_scatter(v, far + last),)])

    def attention_grads(mine):
        mine = mine.reshape(row_sp, 4, head_tp)
        return mine[:, :3].transpose(1, 0, 2), mine[:, 3].T

    def gather(block):
        if near:
            return gather_chain(block, far, last)
        dims = far + last

        def run(block):
            full = in_device_order(cube_gather(block, dims), dims)
            return (full.reshape(n_tp, width, -1),)

        return Chain((block,), [run])

    cond_act = jax.nn.silu(condition).astype(BF)
    cond_rows = lax.dynamic_slice_in_dim(cond_act, my_sp * row_sp, row_sp, axis=1)
    modulation = sum_chain(
        jnp.dot(cond_rows, w_mod, preferred_element_type=F32), [(a, [b]) for a, b in sp_dims]
    )
    place = piece_masks(far, last) if near else None
    chain_s = gather(pack(w_qkv_s, w_o_s))
    chain_t = gather(pack(w_qkv_t, w_o_t))

    def hot_of(ids):
        hot = (ids[..., None] == jnp.arange(clips, dtype=jnp.int32)).astype(BF)
        return jnp.concatenate([hot, hot], axis=-1), jnp.swapaxes(hot, -1, -2)

    first = my_sp * sp_frames + my_tp * frames
    ids_s = lax.dynamic_slice_in_dim(clip_ids, first, frames)
    hot_s, hot_s_t = hot_of(jnp.repeat(ids_s[:, None], PATCHES, axis=1))
    ids_t = jnp.repeat(clip_ids, per_block)
    hot_t, hot_t_t = hot_of(ids_t[None])
    hot_f, hot_f_t = hot_of(
        jnp.repeat(clip_ids, places) if zipped else jnp.tile(ids_t, blocks)
    )
    key = ids_t * per_block + jnp.tile(jnp.arange(per_block, dtype=jnp.int32), all_frames)
    keys = key[:, None], key[None, :]
    meta0 = jnp.stack([0 * my_tp, my_tp, my_sp]).astype(jnp.int32)
    meta_s = jnp.stack([my_tp * frames, my_tp, my_sp]).astype(jnp.int32)

    def exchange(value):
        return lax.all_to_all(value, ("sp", "tp"), 0, 0, tiled=True)

    def to_places(value):
        if zipped:
            return exchange(value)
        split = value.reshape(frames, devices, blocks, per_block, width).transpose(1, 2, 0, 3, 4)
        return exchange(split).transpose(1, 0, 2, 3, 4).reshape(blocks, rows, width)

    def to_frames(value):
        if zipped:
            return exchange(value)
        split = value.reshape(blocks, devices, frames, per_block, width).transpose(1, 0, 2, 3, 4)
        return exchange(split).transpose(2, 0, 1, 3, 4).reshape(frames, PATCHES, width)

    def input_to_places(value):
        split = value.reshape(sp_frames, n_sp, n_tp, places, width)
        split = lax.dynamic_slice_in_dim(split, my_tp, 1, axis=2)[:, :, 0].transpose(1, 0, 2, 3)
        got = lax.all_to_all(split, "sp", 0, 0, tiled=True)
        if not zipped:
            got = got.reshape(all_frames, blocks, per_block, width).transpose(1, 0, 2, 3)
        return got.reshape(blocks * rows, width)

    def split_output(value):
        if not zipped:
            value = value.reshape(blocks, all_frames, per_block, width).transpose(1, 0, 2, 3)
        return lax.all_to_all(
            value.reshape(n_sp, sp_frames, places, width), "sp", 0, 0, tiled=True
        )

    feed_in = w_up, w_down
    for step in range(max(5, len(modulation.steps))):
        chain_s.go()
        modulation.go()
        if step in (2, 3, 4):
            chain_t.go()
        if step == FEED_STEP:
            feed_in = stage([chain_s, chain_t, modulation], *feed_in)
        else:
            stage([chain_s, chain_t, modulation])
    feed = lax.all_gather(jnp.stack([feed_in[0], feed_in[1].T]), ("tp", "sp"), axis=0)
    feed = feed.reshape(n_tp, n_sp, 2, row_sp, -1)
    (modulation,) = modulation.state
    coarse = lax.reduce_precision(modulation, 8, 7)
    mst = jnp.concatenate([coarse, modulation - coarse]).astype(BF)
    mst_s, mst_t, mst_f = (mst[:, i * 3 * width : (i + 1) * 3 * width] for i in range(3))


    own = tokens.reshape(sp_frames, PATCHES, width)
    x1_shape = (devices, frames, places, width) if zipped else (frames, PATCHES, width)
    x1_frames, h1, qkv1, p1, o1, a1 = forward(
        meta_s, own, frames, PATCHES, hot_s, mst_s, None, chain_s.state, place, n_tp, heads,
        x1_shape, BF,
    )
    chain_t.go()
    x1 = to_places(x1_frames)
    x1 = stage([chain_t], x1)
    chain_t.go()
    x1, grad_in = stage([chain_t], x1, grad_out)
    grad_rows = input_to_places(grad_in)
    x2, h2, qkv2, p2, o2, a2 = forward(
        meta0, x1, blocks, rows, hot_t, mst_t, keys, chain_t.state, place, n_tp, heads,
        x1.shape, F32,
    )

    feed_args = x2.reshape(blocks * rows, width), grad_rows, hot_f, hot_f_t, mst_f, feed, masks
    if near:
        *sums, far_terms = feed_half(meta0, *feed_args, None)
        block_out, dx2, dm_f, near_terms = feed_half(meta0, *feed_args, sums)
        out_f = scatter([far_terms, near_terms])
        out_f.go()
        dx2, block_out = stage([out_f], dx2, block_out)
    else:
        *sums, up_one, down_one = feed_half(meta0, *feed_args, None)
        block_out, dx2, dm_f, up_two, down_two = feed_half(meta0, *feed_args, sums)
        pair = [jnp.concatenate(p) for p in ((up_one, up_two), (down_one, down_two))]
        pair = [scatter([terms]).run()[0] for terms in pair]
        out_f = Chain((jnp.concatenate(pair),), [])

    out_f.go()
    block_out = split_output(block_out)
    dx1, dqkv2, da2, dm_t = backward(
        meta0, dx2.reshape(x2.shape), x1, hot_t, hot_t_t, mst_t, a2, qkv2, p2,
        chain_t.state, place, heads,
    )
    dx1_frames = to_frames(dx1)
    dqkv2, block_out = stage([out_f], dqkv2, block_out)
    out_f.go()
    terms_t = weight_grads(meta0, h2, dqkv2, da2, o2, masks, row_sp)
    all_out = lax.all_gather(block_out, "tp", axis=0)
    dx1_frames, terms_t = stage([out_f], dx1_frames, terms_t)

    out_t = scatter(terms_t)
    out_t.go()
    out_f.go()
    dx0, dqkv1, da1, dm_s = backward(
        meta_s, dx1_frames, own, hot_s, hot_s_t, mst_s, a1, qkv1, p1, chain_s.state, place, heads
    )
    dx0, dqkv1, dm_s = stage([out_t, out_f], dx0, dqkv1, dm_s)
    wide = [("sp", list(range(1, sp_bits)))] if near else [("sp", [b]) for a, b in far]
    dm = sum_chain(
        jnp.concatenate([dm_s, dm_t, dm_f], axis=-1),
        [("tp", list(range(tp_bits)))] + [("sp", [b]) for b in range(sp_bits)],
    )
    grad_tokens = lax.all_gather(dx0.reshape(-1, width), "tp", axis=0, tiled=True)
    out_t.go()
    out_f.go()
    dm.go()
    terms_s = weight_grads(meta0, h1, dqkv1, da1, o1, masks, row_sp)
    terms_s, all_out = stage([out_t, out_f, dm], terms_s, all_out)
    out_s = scatter(terms_s)

    def condition_part(low):
        mine = jnp.dot(low, w_mod.T, preferred_element_type=F32)
        spot = jnp.arange(n_sp)[:, None, None] == my_sp
        return sum_chain(jnp.where(spot, mine[None], 0.0), [("sp", [0])] + wide)

    done = {}
    part, step = None, 0
    chains = [out_s, out_t, out_f, dm]
    while part is None or any(c.steps for c in chains + [part]):
        out_s.go()
        if out_t.steps:
            out_t.go()
        elif "t" not in done:
            done["t"] = attention_grads(out_t.state[0])
        if out_f.steps:
            out_f.go()
        elif "f" not in done:
            done["f"] = out_f.state[0][:row_sp], out_f.state[0][row_sp:].T
        if step == 2:
            done["out"] = all_out.transpose(2, 1, 0, 3, 4).reshape(-1, width)
        if dm.steps:
            dm.go()
        elif part is None:
            low = dm.state[0].astype(BF)
            part = condition_part(low)
            done["mod"] = jnp.dot(cond_rows.T, low, preferred_element_type=F32)
        if part is not None:
            part.go()
        if step == TOKENS_STEP:
            done["tokens"] = grad_tokens
        names = sorted(done)
        waits = chains + ([part] if part is not None else [])
        values = stage(waits, [done[n] for n in names])
        done = dict(zip(names, values))
        step += 1
    grad_act = part.state[0].transpose(1, 0, 2).reshape(clips, width)
    unused, silu_pull = jax.vjp(jax.nn.silu, condition)
    grad_condition = silu_pull(grad_act)[0]
    if "t" not in done:
        done["t"] = attention_grads(out_t.state[0])
    sum_qt, sum_ot = done["t"]
    sum_qs, sum_os = attention_grads(out_s.state[0])
    return (
        done["out"],
        done["tokens"],
        grad_condition,
        done["mod"],
        sum_qs,
        sum_os,
        sum_qt,
        sum_ot,
        *done["f"],
    )


def solution(mesh):
    placed = (
        P("sp", None),
        P(),
        P(),
        P("sp", None),
        P(None, "sp", "tp"),
        P("tp", "sp"),
        P(None, "sp", "tp"),
        P("tp", "sp"),
        P("sp", "tp"),
        P("tp", "sp"),
        P("sp", None),
    )
    return jax.shard_map(
        shards,
        mesh=mesh,
        in_specs=placed,
        out_specs=(
            P("sp", None),
            P("sp", None),
            P(),
            P("sp", None),
            P(None, "sp", "tp"),
            P("tp", "sp"),
            P(None, "sp", "tp"),
            P("tp", "sp"),
            P("sp", "tp"),
            P("tp", "sp"),
        ),
        check_vma=False,
    )
```

```python
import functools

import jax
import jax.numpy as jnp
from jax import lax
from jax.experimental import pallas as pl
from jax.experimental.pallas import tpu as pltpu
from jax.sharding import PartitionSpec as P

HD = 64
PATCHES = 256
BLOCK_ROWS = 256
COSTS = (20, 20, 2, 1, 20)
LATE_STEP = -1
DM_EARLY = 0
EPSILON = 1e-06
HIGHEST = lax.Precision.HIGHEST
BF = jnp.bfloat16
F32 = jnp.float32


def bits_of(size):
    return size.bit_length() - 1


def swap(value, axis, bit):
    size = lax.axis_size(axis)
    return lax.ppermute(value, axis, [(i, i ^ (1 << bit)) for i in range(size)])


def swap_far(value, far, mask):
    axis = far[0][0]
    flip = sum(1 << bit for i, (a, bit) in enumerate(far) if mask >> i & 1)
    size = lax.axis_size(axis)
    return lax.ppermute(value, axis, [(i, i ^ flip) for i in range(size)])


def swap_both(value, one, two):
    sizes = lax.axis_size("tp"), lax.axis_size("sp")
    bits = dict([one, two])
    flip = (sizes[1] << bits["tp"]) ^ (1 << bits["sp"])
    return lax.ppermute(value, ("tp", "sp"), [(i, i ^ flip) for i in range(sizes[0] * sizes[1])])


def my_bit(axis, bit):
    return (lax.axis_index(axis) >> bit) & 1


def cube_sum(value, dims):
    for axis, bit in dims:
        value = value + swap(value, axis, bit)
    return value


def cube_gather(block, dims):
    held = block[None]
    for axis, bit in dims:
        other = swap(held, axis, bit)
        high = my_bit(axis, bit) == 1
        held = jnp.concatenate([jnp.where(high, other, held), jnp.where(high, held, other)])
    return held


def cube_scatter(parts, dims):
    for axis, bit in reversed(dims):
        half = parts.shape[0] // 2
        mine = my_bit(axis, bit)
        send = lax.dynamic_slice_in_dim(parts, (1 - mine) * half, half)
        keep = lax.dynamic_slice_in_dim(parts, mine * half, half)
        got = swap(send, axis, bit)
        parts = keep.astype(F32) + got.astype(F32)
        if half > 1:
            parts = parts.astype(BF)
    return parts[0]


def in_device_order(gathered, dims, back=False):
    count = len(dims)
    want = [("tp", b) for b in reversed(range(bits_of(lax.axis_size("tp"))))]
    want += [("sp", b) for b in reversed(range(bits_of(lax.axis_size("sp"))))]
    have = list(reversed(dims))
    tail = gathered.shape[1:]
    if back:
        have, want = want, have
    split = gathered.reshape((2,) * count + tail)
    order = [have.index(w) for w in want]
    split = split.transpose(order + [count + i for i in range(len(tail))])
    return split.reshape((2**count,) + tail)


VMEM_BYTES = 52 * 1024 * 1024


def cost(micros):
    return pl.CostEstimate(flops=micros * 10**9, bytes_accessed=2**10, transcendentals=0)


def after(value, *others):
    return lax.optimization_barrier((value,) + others)[0]


class Chain:
    def __init__(self, state, steps):
        self.state, self.steps = tuple(state), list(steps)

    def go(self):
        if self.steps:
            self.state = tuple(self.steps.pop(0)(*self.state))

    def run(self):
        while self.steps:
            self.go()
        return self.state


def stage(chains, *values):
    states, values = lax.optimization_barrier(([c.state for c in chains], values))
    for chain, state in zip(chains, states):
        chain.state = tuple(state)
    return values if len(values) != 1 else values[0]


def gather_chain(block, far, last):
    def far_step(held):
        return (jnp.concatenate([held] + [swap_far(held, far, m) for m in range(1, 1 << len(far))]),)

    def split(held):
        half = held.shape[1] // 2
        one, two = held[:, :half], held[:, half:]
        return (
            jnp.concatenate([one, swap(one, *last[0])]),
            jnp.concatenate([two, swap(two, *last[1])]),
        )

    def join(one, two):
        return (jnp.concatenate([one, swap(one, *last[1]), two, swap(two, *last[0])]),)

    def final(held):
        return (held, swap(held, *last[2]))

    return Chain((block[None],), [far_step, split, join, final])


def scatter_chain(other, mine, far, last, direct=False, early=False, by_bits=False):
    def add(left, *rights):
        return sum((r.astype(F32) for r in rights), left.astype(F32))

    def first(other, mine):
        total = add(mine, swap(other, *last[2])).astype(BF)
        count, rows = total.shape[0], total.shape[1]
        if direct:
            parts = total.reshape((2, 2, count // 4, rows) + total.shape[2:])
            return parts[0, 0], parts[0, 1], parts[1, 0], parts[1, 1]
        total = total.reshape((2, 2, count // 4, 2, rows // 2) + total.shape[2:])
        one, two = total[:, :, :, 0], total[:, :, :, 1]
        return one[0], one[1], two[:, 0], two[:, 1]

    def second(keep_one, send_one, keep_two, send_two):
        return keep_one, swap(send_one, *last[1]), keep_two, swap(send_two, *last[0])

    def second_sum(keep_one, got_one, keep_two, got_two):
        one = add(keep_one, got_one).astype(BF)
        two = add(keep_two, got_two).astype(BF)
        return one[0], one[1], two[0], two[1]

    def third(keep_one, send_one, keep_two, send_two):
        one = add(keep_one, swap(send_one, *last[0])).astype(BF)
        two = add(keep_two, swap(send_two, *last[1])).astype(BF)
        both = jnp.concatenate([one, two], axis=1)
        return tuple(both[m] for m in range(both.shape[0]))

    def at_once(keep, send_near, send_far, send_both):
        got = (
            swap(send_near, *last[0]),
            swap(send_far, *last[1]),
            swap_both(send_both, last[0], last[1]),
        )
        total = add(keep, *got).astype(BF)
        return tuple(total[m] for m in range(total.shape[0]))

    def far_step(*parts):
        return (add(parts[0], *[swap_far(p, far, m + 1) for m, p in enumerate(parts[1:])]),)

    def bit_step(bit):
        def run(*parts):
            half = len(parts) // 2
            sent = swap(jnp.stack(parts[half:]), *far[bit])
            sums = [add(p, g) for p, g in zip(parts[:half], sent)]
            return (sums[0],) if half == 1 else tuple(v.astype(BF) for v in sums)

        return run

    far_steps = [bit_step(b) for b in reversed(range(len(far)))] if by_bits else [far_step]

    def both_seconds(*state):
        return second_sum(*second(*state))

    if direct:
        steps = [first, at_once]
    elif early:
        steps = [first, second, second_sum, third]
    else:
        steps = [first, both_seconds, third]
    return Chain((other, mine), steps + far_steps)


def sum_chain(value, dims):
    def step(axis, bits):
        masks = [0]
        for bit in bits:
            masks += [m | 1 << bit for m in masks]
        size = lax.axis_size(axis)

        def run(value):
            others = [lax.ppermute(value, axis, [(i, i ^ m) for i in range(size)]) for m in masks[1:]]
            return (sum(others, value),)

        return run

    return Chain((value,), [step(*d) for d in dims])


def dims_masks(dims):
    masks = []
    for m in range(2 ** len(dims)):
        flip = {"tp": 0, "sp": 0}
        for place, (axis, bit) in enumerate(dims):
            flip[axis] |= ((m >> place) & 1) << bit
        masks.append((flip["tp"], flip["sp"]))
    return masks


def tp_flip(last, step):
    return (step % 2) << last[1][1] | (1 - step // 2) << last[2][1]


def tp_at(place, step, meta):
    if place is None:
        return step
    return meta[1] ^ tp_flip(place[1], step)


def dot(left, right, left_dim, right_dim):
    return lax.dot_general(
        left, right, (((left_dim,), (right_dim,)), ((), ())), preferred_element_type=F32
    )


def norm_rows(operand):
    centred = operand - jnp.mean(operand, axis=-1, keepdims=True)
    inverse = lax.rsqrt(jnp.mean(centred * centred, axis=-1, keepdims=True) + EPSILON)
    return (centred * inverse, inverse)


def norm_back(incoming, normed, inverse):
    first_mean = jnp.mean(incoming, axis=-1, keepdims=True)
    second_mean = jnp.mean(incoming * normed, axis=-1, keepdims=True)
    return inverse * (incoming - first_mean - normed * second_mean)


def params(count=1):
    return pltpu.CompilerParams(
        dimension_semantics=("arbitrary",) * count, vmem_limit_bytes=VMEM_BYTES
    )


def whole(shape):
    zeros = (0,) * len(shape)
    return pl.BlockSpec(shape, lambda g, meta: zeros, pipeline_mode=pl.Buffered(1))


def step_weights(meta, pieces, place, step, target):
    if place is None:
        return pieces[0]
    far, last = place
    near_count = 1 << len(far)
    half = pieces[0].shape[1]
    index = step % 2

    def fill(piece):
        for m in range(2 * near_count):
            z, y = m % near_count, m // near_count
            flip = sum(1 << bit for i, (a, bit) in enumerate(far) if z >> i & 1)
            flip |= y << last[0][1]
            at = pl.multiple_of((meta[2] ^ flip) * (2 * half), 2 * half)
            target[pl.ds(at, half), :] = piece[index * 2 * near_count + m]
            target[pl.ds(at + half, half), :] = piece[
                4 * near_count + y * 2 * near_count + index * near_count + z
            ]

    @pl.when(step // 2 == 1)
    def _():
        fill(pieces[0])

    @pl.when(step // 2 == 0)
    def _():
        fill(pieces[1])

    return target


def columns(weights, start, stop):
    if len(weights.shape) == 2:
        return weights[:, start:stop]
    if len(weights.shape) == 3:
        return weights[0, :, start:stop]
    return weights[0, :, 0, :, start:stop].reshape(-1, stop - start)


def split_places(pair):
    count, width = pair.shape[0], pair.shape[3]
    one, two = pair[:, 0], pair[:, 1]
    upper = lax.broadcasted_iota(jnp.int32, one.shape, 1) < 4
    left = jnp.where(upper, one, pltpu.roll(two, 4, 1))
    right = jnp.where(upper, pltpu.roll(one, 4, 1), two)
    return left.reshape(count * 8, width), right.reshape(count * 8, width)


def join_places(left, right):
    count, width = left.shape[0] // 8, left.shape[1]
    left, right = left.reshape(count, 8, width), right.reshape(count, 8, width)
    upper = lax.broadcasted_iota(jnp.int32, left.shape, 1) < 4
    one = jnp.where(upper, left, pltpu.roll(right, 4, 1))
    two = jnp.where(upper, pltpu.roll(left, 4, 1), right)
    return one, two


def blocks_of(x, groups):
    if len(x.shape) == 4 and groups == 2 and x.shape[1:3] == (2, 8):
        return list(split_places(x[...].astype(F32)))
    return [x[g].astype(F32) for g in range(groups)]


def forward_kernel(place, heads, masked, zipped, meta, x, hot, mst, key_r, key_c, *refs):
    pieces = refs[: 1 if place is None else 2]
    x_out, h_out, qkv_out, p_out, o_out, a_out, w, acc = refs[len(pieces) :]
    groups, rows, width = h_out.shape
    head_tp = heads * HD
    step = pl.program_id(0)

    def modulation(g, i):
        return dot(hot[g % hot.shape[0]], mst[:, i * width : (i + 1) * width], 1, 0)

    @pl.when(step == 0)
    def _():
        for g, xin in enumerate(blocks_of(x, groups)):
            normed = norm_rows(xin)[0]
            h_out[g] = (normed * (1.0 + modulation(g, 1)) + modulation(g, 0)).astype(BF)

    wt = step_weights(meta, pieces, place, step, w)
    bias = jnp.where(key_r[...] == key_c[...], 0.0, -1e30) if masked else None
    h = h_out[...].reshape(groups * rows, width)
    proj = dot(h, columns(wt, 0, 3 * head_tp), 1, 0).astype(BF)
    qkv_out[:, 0] = proj.reshape(groups, rows, 3 * head_tp)
    mixed = []
    for g in range(groups):
        outs = []
        for j in range(heads):
            q, k, v = (
                proj[g * rows : (g + 1) * rows, i * head_tp + j * HD : i * head_tp + (j + 1) * HD]
                for i in range(3)
            )
            scores = dot(k, q * jnp.asarray(0.125, BF), 1, 1)
            if masked:
                scores = scores + bias
            e = jnp.exp(scores - jnp.max(scores, axis=0, keepdims=True))
            p = (e * (1.0 / jnp.sum(e, axis=0, keepdims=True))).astype(BF)
            p_out[g, j] = p
            outs.append(dot(v, p, 0, 0))
        mixed.append(jnp.concatenate(outs, axis=0).T.astype(BF))
        o_out[g, 0] = mixed[-1]
    o = jnp.concatenate(mixed, axis=0)
    part = dot(o, columns(wt, 3 * head_tp, 4 * head_tp), 1, 1)

    @pl.when(step == 0)
    def _():
        acc[...] = part

    @pl.when(step > 0)
    def _():
        acc[...] += part

    @pl.when(step == pl.num_programs(0) - 1)
    def _():
        new = []
        for g, xin in enumerate(blocks_of(x, groups)):
            total = acc[g * rows : (g + 1) * rows, :]
            a_out[g] = total.astype(BF)
            new.append(xin + modulation(g, 2) * total)
        if zipped:
            one, two = join_places(*new)
            x_out[:, 0], x_out[:, 1] = one.astype(x_out.dtype), two.astype(x_out.dtype)
        else:
            for g in range(groups):
                if len(x_out.shape) == 4:
                    shape = (x_out.shape[0],) + x_out.shape[2:]
                    x_out[:, g] = new[g].reshape(shape).astype(x_out.dtype)
                else:
                    x_out[g] = new[g].astype(x_out.dtype)


def weight_specs(pieces, place):
    if place is not None:
        return [whole(p.shape) for p in pieces]
    (full,) = pieces
    if full.ndim == 5:
        block = (1, full.shape[1], 1) + full.shape[3:]
        return [pl.BlockSpec(block, lambda g, meta: (g, 0, 0, 0, 0))]
    return [pl.BlockSpec((1,) + full.shape[1:], lambda g, meta: (g, 0, 0))]


def head_spec(place, groups, *shape):
    zeros = (0,) * (len(shape) - 1)
    return pl.BlockSpec((groups,) + shape, lambda g, meta: (0, tp_at(place, g, meta)) + zeros)


def fixed(shape):
    zeros = (0,) * len(shape)
    return pl.BlockSpec(shape, lambda g, meta: zeros)


def rows_spec(x, groups, zipped):
    if zipped or x.ndim == 4:
        return whole(x.shape)
    return pl.BlockSpec(
        (groups,) + x.shape[1:], lambda g, meta: (meta[0] // groups, 0, 0),
        pipeline_mode=pl.Buffered(1),
    )


def forward(meta, x, groups, rows, hot, mst, keys, pieces, place, n_tp, heads, x_shape, out_dtype):
    width = x.shape[-1]
    lanes = 4 * heads * HD
    masked = keys is not None
    zipped = x.ndim == 4
    if keys is None:
        keys = jnp.zeros((8, 1), jnp.int32), jnp.zeros((1, 128), jnp.int32)
    return pl.pallas_call(
        functools.partial(forward_kernel, place, heads, masked, zipped),
        out_shape=[
            jax.ShapeDtypeStruct(x_shape, out_dtype),
            jax.ShapeDtypeStruct((groups, rows, width), BF),
            jax.ShapeDtypeStruct((groups, n_tp, rows, 3 * heads * HD), BF),
            jax.ShapeDtypeStruct((groups, n_tp * heads, rows, rows), BF),
            jax.ShapeDtypeStruct((groups, n_tp, rows, heads * HD), BF),
            jax.ShapeDtypeStruct((groups, rows, width), BF),
        ],
        grid_spec=pltpu.PrefetchScalarGridSpec(
            num_scalar_prefetch=1,
            grid=(n_tp,),
            in_specs=[
                rows_spec(x, groups, zipped),
                whole(hot.shape),
                whole(mst.shape),
                whole(keys[0].shape),
                whole(keys[1].shape),
            ]
            + weight_specs(pieces, place),
            out_specs=[
                fixed(x_shape),
                fixed((groups, rows, width)),
                head_spec(place, groups, 1, rows, 3 * heads * HD),
                head_spec(place, groups, heads, rows, rows),
                head_spec(place, groups, 1, rows, heads * HD),
                fixed((groups, rows, width)),
            ],
            scratch_shapes=[
                pltpu.VMEM((width, lanes), BF),
                pltpu.VMEM((groups * rows, width), F32),
            ],
        ),
        compiler_params=params(),
        cost_estimate=cost(COSTS[0]),
    )(meta, x, hot, mst, *keys, *pieces)


def grads_in(dx, groups, rows):
    if len(dx.shape) == 4 and dx.shape[1] == groups and dx.shape[0] * dx.shape[2] == rows:
        return [dx[:, g].astype(F32).reshape(rows, dx.shape[3]) for g in range(groups)]
    return [dx[g].astype(F32) for g in range(groups)]


def heads_back(heads, w, da, qkv, p, groups, rows):
    head_tp = heads * HD
    do = dot(da, columns(w, 3 * head_tp, 4 * head_tp), 1, 0).astype(BF)
    out = []
    for g in range(groups):
        got = [[], [], []]
        for j in range(heads):
            q, k, v = (
                qkv[g, 0, :, i * head_tp + j * HD : i * head_tp + (j + 1) * HD] for i in range(3)
            )
            dop = do[g * rows : (g + 1) * rows, j * HD : (j + 1) * HD]
            prob = p[g, j]
            dp = dot(v, dop, 1, 1)
            prob32 = prob.astype(F32)
            prod = prob32 * dp
            ds = (prod - prob32 * jnp.sum(prod, axis=0, keepdims=True)).astype(BF)
            got[0].append(dot(k, ds, 0, 0))
            got[1].append(dot(ds, q, 1, 0))
            got[2].append(dot(prob, dop, 1, 0))
        dq = jnp.concatenate(got[0], axis=0).T * 0.125
        dk = jnp.concatenate(got[1], axis=1) * 0.125
        out.append(jnp.concatenate([dq, dk] + got[2], axis=1).astype(BF))
    return out[0] if groups == 1 else jnp.concatenate(out, axis=0)


def finish_rows(hot, hot_t, mst, x, a, grads, dh, dm_out, groups):
    rows, width = a.shape[1], a.shape[2]
    sums = None
    out = []
    for g, xin in enumerate(blocks_of(x, groups)):
        at = slice(g * rows, (g + 1) * rows)
        gain = 1.0 + dot(hot[g % hot.shape[0]], mst[:, width : 2 * width], 1, 0)
        normed, inverse = norm_rows(xin)
        part = dh[at, :]
        grad = grads[g]
        out.append(grad + norm_back(part * gain, normed, inverse))
        new = [
            dot(hot_t[g % hot.shape[0]], value.astype(BF), 1, 0)
            for value in (part, part * normed, grad * a[g].astype(F32))
        ]
        sums = new if sums is None else [s + n for s, n in zip(sums, new)]
    for i in range(3):
        dm_out[:, i * width : (i + 1) * width] = sums[i]
    return out


def half_specs(half, shape):
    zeros = (0,) * len(shape)
    return [
        pl.BlockSpec((1,) + shape, lambda g, meta: (jnp.minimum(g, half - 1),) + zeros),
        pl.BlockSpec((1,) + shape, lambda g, meta: (jnp.maximum(g - half, 0),) + zeros),
    ]


def store_grads(masks, meta, step, first, second, blocks, outs):
    wide = first.shape[1]
    if masks is None:
        outs[0][0, :, :wide] = first
        outs[0][0, :, wide:] = second
        return
    blocks[:, :wide] = first
    blocks[:, wide:] = second
    half = pl.num_programs(0) // 2

    @pl.when(step < half)
    def _():
        store_blocks(meta, masks, blocks, outs[0].at[0])

    @pl.when(step >= half)
    def _():
        store_blocks(meta, masks, blocks, outs[1].at[0])


def grads_out(masks, n_tp, width, row_sp, lanes):
    if masks is None:
        out_shape = [jax.ShapeDtypeStruct((n_tp, width, lanes), BF)]
        return out_shape, [pl.BlockSpec((1, width, lanes), lambda g, meta: (g, 0, 0))]
    half = n_tp // 2
    shape = (len(masks) // n_tp, row_sp, lanes)
    return [jax.ShapeDtypeStruct((half,) + shape, BF)] * 2, half_specs(half, shape)


def back_kernel(masks, heads, meta, dx, x, hot, hot_t, mst, a, h, o, qkv, p, w, *refs):
    dx_out, dm_out, *outs, dh, h_t, da, da_t, blocks = refs
    groups, rows, width = a.shape
    head_tp = heads * HD
    step = pl.program_id(0)
    zipped = len(x.shape) == 4

    @pl.when(step == 0)
    def _():
        for g, grad in enumerate(blocks_of(dx, groups)):
            at = slice(g * rows, (g + 1) * rows)
            gate = dot(hot[g % hot.shape[0]], mst[:, 2 * width :], 1, 0)
            low = (gate * grad).astype(BF)
            da[at, :] = low
            da_t[:, at] = low.T
            h_t[:, at] = h[g].T

    dqkv = heads_back(heads, w, da[...], qkv, p, groups, rows)
    part = dot(dqkv, columns(w, 0, 3 * head_tp), 1, 1)
    first = dot(h_t[...], dqkv, 1, 0).astype(BF)
    second = dot(da_t[...], o[...].reshape(groups * rows, head_tp), 1, 0).astype(BF)
    store_grads(masks, meta, step, first, second, blocks, outs)

    @pl.when(step == 0)
    def _():
        dh[...] = part

    @pl.when(step > 0)
    def _():
        dh[...] += part

    @pl.when(step == pl.num_programs(0) - 1)
    def _():
        grads = blocks_of(dx, groups)
        new = finish_rows(hot, hot_t, mst, x, a, grads, dh, dm_out, groups)
        if zipped:
            one, two = join_places(*new)
            dx_out[:, 0], dx_out[:, 1] = one.astype(BF), two.astype(BF)
        else:
            for g in range(groups):
                dx_out[g] = new[g].astype(BF)


def backward(meta, dx, x, hot, hot_t, mst, a, h, o, qkv, p, pieces, place, masks, row_sp, heads):
    groups, n_tp, rows = qkv.shape[:3]
    width = a.shape[2]
    clips = hot_t.shape[1]
    lanes = 4 * heads * HD
    out_shape, out_specs = grads_out(masks, n_tp, width, row_sp, lanes)
    (full,) = pieces
    ahead = (1, full.shape[1], 1) if full.ndim == 5 else (1,)
    block = ahead + full.shape[-2:]
    zeros = (0,) * (len(block) - 1)
    return pl.pallas_call(
        functools.partial(back_kernel, masks, heads),
        out_shape=[
            jax.ShapeDtypeStruct(x.shape, BF),
            jax.ShapeDtypeStruct((clips, 3 * width), F32),
        ]
        + out_shape,
        grid_spec=pltpu.PrefetchScalarGridSpec(
            num_scalar_prefetch=1,
            grid=(n_tp,),
            in_specs=[
                whole(dx.shape),
                whole(x.shape),
                whole(hot.shape),
                whole(hot_t.shape),
                whole(mst.shape),
                whole(a.shape),
                whole(h.shape),
                head_spec(place, groups, 1, rows, heads * HD),
                head_spec(place, groups, 1, rows, 3 * heads * HD),
                head_spec(place, groups, heads, rows, rows),
                pl.BlockSpec(block, lambda g, meta: (tp_at(place, g, meta),) + zeros),
            ],
            out_specs=[fixed(x.shape), fixed((clips, 3 * width))] + out_specs,
            scratch_shapes=[
                pltpu.VMEM((groups * rows, width), F32),
                pltpu.VMEM((width, groups * rows), BF),
                pltpu.VMEM((groups * rows, width), BF),
                pltpu.VMEM((width, groups * rows), BF),
                pltpu.VMEM((width, lanes), BF),
            ],
        ),
        compiler_params=params(),
        cost_estimate=cost(COSTS[1]),
    )(meta, dx, x, hot, hot_t, mst, a, h, o, qkv, p, full)


def back_grads_kernel(place, masks, heads, meta, dx, hot, mst, h, o, qkv, p, *refs):
    pieces = refs[: 1 if place is None else 2]
    dqkv_out, *outs, w, h_t, da, da_t, blocks = refs[len(pieces) :]
    groups, rows, width = h.shape
    head_tp = heads * HD
    step = pl.program_id(0)

    @pl.when(step == 0)
    def _():
        for g, grad in enumerate(grads_in(dx, groups, rows)):
            at = slice(g * rows, (g + 1) * rows)
            gate = dot(hot[g % hot.shape[0]], mst[:, 2 * width :], 1, 0)
            low = (gate * grad).astype(BF)
            da[at, :] = low
            da_t[:, at] = low.T
            h_t[:, at] = h[g].T

    wt = step_weights(meta, pieces, place, step, w)
    dqkv = heads_back(heads, wt, da[...], qkv, p, groups, rows)
    dqkv_out[:, 0] = dqkv.reshape(groups, rows, 3 * head_tp)
    first = dot(h_t[...], dqkv, 1, 0).astype(BF)
    second = dot(da_t[...], o[...].reshape(groups * rows, head_tp), 1, 0).astype(BF)
    store_grads(masks, meta, step, first, second, blocks, outs)


def backward_grads(meta, dx, hot, mst, h, o, qkv, p, pieces, place, masks, row_sp, heads):
    groups, n_tp, rows = qkv.shape[:3]
    width = h.shape[2]
    lanes = 4 * heads * HD
    out_shape, out_specs = grads_out(masks, n_tp, width, row_sp, lanes)
    return pl.pallas_call(
        functools.partial(back_grads_kernel, place, masks, heads),
        out_shape=[jax.ShapeDtypeStruct(qkv.shape, BF)] + out_shape,
        grid_spec=pltpu.PrefetchScalarGridSpec(
            num_scalar_prefetch=1,
            grid=(n_tp,),
            in_specs=[
                whole(dx.shape),
                whole(hot.shape),
                whole(mst.shape),
                whole(h.shape),
                head_spec(place, groups, 1, rows, heads * HD),
                head_spec(place, groups, 1, rows, 3 * heads * HD),
                head_spec(place, groups, heads, rows, rows),
            ]
            + weight_specs(pieces, place),
            out_specs=[head_spec(place, groups, 1, rows, 3 * heads * HD)] + out_specs,
            scratch_shapes=[
                pltpu.VMEM((width, lanes), BF),
                pltpu.VMEM((width, groups * rows), BF),
                pltpu.VMEM((groups * rows, width), BF),
                pltpu.VMEM((width, groups * rows), BF),
                pltpu.VMEM((width, lanes), BF),
            ],
        ),
        compiler_params=params(),
        cost_estimate=cost(COSTS[1]),
    )(meta, dx, hot, mst, h, o, qkv, p, *pieces)


def input_back_kernel(place, heads, meta, dx, x, hot, hot_t, mst, a, dqkv, *refs):
    pieces = refs[: 1 if place is None else 2]
    dx_out, dm_out, w, dh = refs[len(pieces) :]
    groups, rows, width = a.shape
    head_tp = heads * HD
    step = pl.program_id(0)
    wt = step_weights(meta, pieces, place, step, w)
    all_rows = dqkv[...].reshape(groups * rows, 3 * head_tp)
    part = dot(all_rows, columns(wt, 0, 3 * head_tp), 1, 1)

    @pl.when(step == 0)
    def _():
        dh[...] = part

    @pl.when(step > 0)
    def _():
        dh[...] += part

    @pl.when(step == pl.num_programs(0) - 1)
    def _():
        grads = grads_in(dx, groups, rows)
        new = finish_rows(hot, hot_t, mst, x, a, grads, dh, dm_out, groups)
        for g in range(groups):
            dx_out[g] = new[g].astype(BF)


def input_back(meta, dx, x, hot, hot_t, mst, a, dqkv, pieces, place, heads):
    groups, n_tp, rows = dqkv.shape[:3]
    width = a.shape[2]
    clips = hot_t.shape[1]
    return pl.pallas_call(
        functools.partial(input_back_kernel, place, heads),
        out_shape=[
            jax.ShapeDtypeStruct(a.shape, BF),
            jax.ShapeDtypeStruct((clips, 3 * width), F32),
        ],
        grid_spec=pltpu.PrefetchScalarGridSpec(
            num_scalar_prefetch=1,
            grid=(n_tp,),
            in_specs=[
                whole(dx.shape),
                rows_spec(x, groups, False),
                whole(hot.shape),
                whole(hot_t.shape),
                whole(mst.shape),
                whole(a.shape),
                head_spec(place, groups, 1, rows, 3 * heads * HD),
            ]
            + weight_specs(pieces, place),
            out_specs=[fixed(a.shape), fixed((clips, 3 * width))],
            scratch_shapes=[
                pltpu.VMEM((width, 4 * heads * HD), BF),
                pltpu.VMEM((groups * rows, width), F32),
            ],
        ),
        compiler_params=params(),
        cost_estimate=cost(COSTS[4]),
    )(meta, dx, x, hot, hot_t, mst, a, dqkv, *pieces)


def store_blocks(meta, masks, scratch, target):
    count, rows = target.shape[0], target.shape[1]
    for place in range(count):
        at = pl.multiple_of((meta[2] ^ masks[place][1]) * rows, rows)
        target[place] = scratch[pl.ds(at, rows), :]


def tp_of(masks, n_tp, g, meta):
    if masks is None:
        return g
    flips = [masks[i * (len(masks) // n_tp)][0] for i in range(n_tp)]
    flips = flips[n_tp // 2 :] + flips[: n_tp // 2]
    flip = 0
    for i, value in enumerate(flips):
        flip = jnp.where(g == i, value, flip)
    return meta[1] ^ flip


GELU_A = 0.7978845608028654
GELU_B = 0.044715


def feed_kernel(masks, last_call, meta, x2, dy, hot, hot_t, mst, up, down, *refs):
    if last_call:
        acc_in, dh_in, out, dx_out, dm_out, *grads, h3, da3, h3_t, da3_t, acc, dh, blocks = refs
    else:
        acc, dh, *grads, h3, da3, h3_t, da3_t, blocks = refs
    width = x2.shape[1]
    step = pl.program_id(0)

    def modulation(i):
        return dot(hot[...], mst[:, i * width : (i + 1) * width], 1, 0)

    @pl.when(step == 0)
    def _():
        normed = norm_rows(x2[...])[0]
        h3[...] = (normed * (1.0 + modulation(1)) + modulation(0)).astype(BF)
        da3[...] = (modulation(2) * dy[...].astype(F32)).astype(BF)
        h3_t[...] = h3[...].T
        da3_t[...] = da3[...].T
        if last_call:
            acc[...], dh[...] = acc_in[...], dh_in[...]
        else:
            acc[...] = jnp.zeros_like(acc)
            dh[...] = jnp.zeros_like(dh)

    wu = up[...].reshape(width, -1)
    wd = down[...].reshape(width, -1)
    u = dot(h3[...], wu, 1, 0)
    square = u * u
    th = jnp.tanh(GELU_A * (u + GELU_B * (square * u)))
    g = (0.5 * u * (1.0 + th)).astype(BF)
    slope = 0.5 * (1.0 + th) + (0.5 * GELU_A) * u * (1.0 - th * th) * (
        1.0 + (3.0 * GELU_B) * square
    )
    dg = dot(da3[...], wd, 1, 0)
    du = (dg * slope).astype(BF)
    acc[...] += dot(g, wd, 1, 1)
    dh[...] += dot(du, wu, 1, 1)
    grad_up = dot(h3_t[...], du, 1, 0).astype(BF)
    grad_down = dot(da3_t[...], g, 1, 0).astype(BF)
    if masks is None:
        grads[0][0], grads[1][0] = grad_up, grad_down
    else:
        for i, value in enumerate((grad_up, grad_down)):
            blocks[...] = value
            store_blocks(meta, masks, blocks, grads[0].at[0, :, i])

    if last_call:

        @pl.when(step == pl.num_programs(0) - 1)
        def _():
            grad = dy[...].astype(F32)
            a3 = acc[...]
            xin = x2[...]
            normed, inverse = norm_rows(xin)
            out[...] = (xin + modulation(2) * a3).astype(BF)
            dh3 = dh[...]
            dx_out[...] = grad + norm_back(dh3 * (1.0 + modulation(1)), normed, inverse)
            for i, value in enumerate([dh3, dh3 * normed, grad * a3]):
                dm_out[:, i * width : (i + 1) * width] = dot(hot_t[...], value.astype(BF), 1, 0)


def feed_half(meta, x2, dy, hot, hot_t, mst, weights, masks, sums):
    rows, width = x2.shape
    n_tp, n_sp, unused, row_sp, units = weights.shape
    clips = hot_t.shape[0]
    half = n_tp // 2
    last_call = sums is not None
    start = half if last_call else 0
    at = lambda g, meta: tp_of(masks, n_tp, g + start, meta)
    if masks is None:
        blocked = weights.transpose(2, 0, 1, 3, 4).reshape(3, n_tp, width, units)
        up, down = blocked[1], blocked[2]
        specs = [pl.BlockSpec((1, width, units), lambda g, meta: (g + start, 0, 0))] * 2
        grad_shapes = [(half, width, units)] * 2
    else:
        up = down = weights
        specs = [
            pl.BlockSpec(
                (1, n_sp, 1, row_sp, units), lambda g, meta, i=i: (at(g, meta), 0, i, 0, 0)
            )
            for i in (1, 2)
        ]
        grad_shapes = [(half, n_sp, 2, row_sp, units)]
    zeros = (0,) * (len(grad_shapes[0]) - 1)
    grad_spec = pl.BlockSpec((1,) + grad_shapes[0][1:], lambda g, meta: (g,) + zeros)
    plain = lambda s: pl.BlockSpec(s, lambda g, meta: (0, 0))
    total = pltpu.VMEM((rows, width), F32)
    kept = [pltpu.VMEM((rows, width), BF)] * 2 + [pltpu.VMEM((width, rows), BF)] * 2
    if last_call:
        out_types = [((rows, width), BF), ((rows, width), F32), ((clips, 3 * width), F32)]
        scratch = kept + [total, total]
    else:
        out_types = [((rows, width), F32), ((rows, width), F32)]
        scratch = kept
    return pl.pallas_call(
        functools.partial(feed_kernel, masks, last_call),
        out_shape=[jax.ShapeDtypeStruct(*t) for t in out_types]
        + [jax.ShapeDtypeStruct(g, BF) for g in grad_shapes],
        grid_spec=pltpu.PrefetchScalarGridSpec(
            num_scalar_prefetch=1,
            grid=(half,),
            in_specs=[
                whole(x2.shape),
                whole(dy.shape),
                whole(hot.shape),
                whole(hot_t.shape),
                whole(mst.shape),
            ]
            + specs
            + ([whole(x2.shape)] * 2 if last_call else []),
            out_specs=[plain(t[0]) for t in out_types] + [grad_spec] * len(grad_shapes),
            scratch_shapes=scratch + [pltpu.VMEM((width, units), BF)],
        ),
        compiler_params=params(),
        cost_estimate=cost(COSTS[3]),
    )(meta, x2, dy, hot, hot_t, mst, up, down, *(sums or ()))


def shards(
    tokens, condition, clip_ids, w_mod, w_qkv_s, w_o_s, w_qkv_t, w_o_t, w_up, w_down, grad_out
):
    n_tp, n_sp = lax.axis_size("tp"), lax.axis_size("sp")
    devices = n_tp * n_sp
    my_tp, my_sp = lax.axis_index("tp"), lax.axis_index("sp")
    width = tokens.shape[1]
    sp_frames = tokens.shape[0] // PATCHES
    frames = sp_frames // n_tp
    all_frames = sp_frames * n_sp
    places = PATCHES // devices
    per_block = max(1, min(places, BLOCK_ROWS // all_frames))
    blocks = places // per_block
    rows = all_frames * per_block
    clips = condition.shape[0]
    head_tp = w_o_s.shape[0]
    heads = head_tp // HD
    row_sp = w_up.shape[0]
    zipped = (frames, per_block, blocks) == (2, 4, 2)

    sp_bits = bits_of(n_sp)
    tp_bits = bits_of(n_tp)
    far = [("sp", b) for b in reversed(range(1, sp_bits))]
    last = [("sp", 0), ("tp", 1), ("tp", 0)]
    every = [("tp", b) for b in range(tp_bits)] + [("sp", b) for b in range(sp_bits)]
    sp_dims = [("sp", b) for b in range(sp_bits)]
    near = row_sp % 32 == 0

    def pack(w_qkv, w_o):
        flat = w_qkv.transpose(1, 0, 2).reshape(row_sp, -1)
        return jnp.concatenate([flat, w_o.T], axis=1)

    masks = dims_masks(far + last) if near else None

    def scatter(terms, **how):
        if near:
            other, mine = (v.reshape((devices // 2, -1) + v.shape[-1:]) for v in terms)
            return scatter_chain(other, mine, far, last, **how)
        terms = jnp.concatenate(terms)
        terms = terms.reshape((devices, -1) + terms.shape[-1:])
        terms = in_device_order(terms, far + last, back=True)
        return Chain((terms,), [lambda v: (cube_scatter(v, far + last),)])

    def attention_grads(mine):
        mine = mine.reshape(row_sp, 4, head_tp)
        return mine[:, :3].transpose(1, 0, 2), mine[:, 3].T

    def gather(block):
        if near:
            return gather_chain(block, far, last)
        dims = far + last

        def run(block):
            full = in_device_order(cube_gather(block, dims), dims)
            return (full.reshape(n_tp, width, -1),)

        return Chain((block,), [run])

    cond_act = jax.nn.silu(condition).astype(BF)
    cond_rows = lax.dynamic_slice_in_dim(cond_act, my_sp * row_sp, row_sp, axis=1)
    wide = [("sp", [0]), ("sp", list(range(1, sp_bits)))] if near else [("sp", [b]) for a, b in sp_dims]
    modulation = sum_chain(jnp.dot(cond_rows, w_mod, preferred_element_type=F32), wide)
    place = (far, last) if near else None
    chain_s = gather(pack(w_qkv_s, w_o_s))
    late = jnp.stack([pack(w_qkv_t, w_o_t), w_up, w_down.T])

    def hot_of(ids):
        hot = (ids[..., None] == jnp.arange(clips, dtype=jnp.int32)).astype(BF)
        return jnp.concatenate([hot, hot], axis=-1), jnp.swapaxes(hot, -1, -2)

    first = my_sp * sp_frames + my_tp * frames
    ids_s = lax.dynamic_slice_in_dim(clip_ids, first, frames)
    hot_s, hot_s_t = hot_of(jnp.repeat(ids_s[:, None], PATCHES, axis=1))
    ids_t = jnp.repeat(clip_ids, per_block)
    hot_t, hot_t_t = hot_of(ids_t[None])
    hot_f, hot_f_t = hot_of(
        jnp.repeat(clip_ids, places) if zipped else jnp.tile(ids_t, blocks)
    )
    key = ids_t * per_block + jnp.tile(jnp.arange(per_block, dtype=jnp.int32), all_frames)
    keys = key[:, None], key[None, :]
    meta0 = jnp.stack([0 * my_tp, my_tp, my_sp]).astype(jnp.int32)
    meta_s = jnp.stack([my_tp * frames, my_tp, my_sp]).astype(jnp.int32)

    def exchange(value):
        return lax.all_to_all(value, ("sp", "tp"), 0, 0, tiled=True)

    def to_places(value):
        if zipped:
            return exchange(value)
        split = value.reshape(frames, devices, blocks, per_block, width).transpose(1, 2, 0, 3, 4)
        return exchange(split).transpose(1, 0, 2, 3, 4).reshape(blocks, rows, width)

    def to_frames(value):
        if zipped:
            return exchange(value)
        split = value.reshape(blocks, devices, frames, per_block, width).transpose(1, 0, 2, 3, 4)
        return exchange(split).transpose(2, 0, 1, 3, 4).reshape(frames, PATCHES, width)

    def input_to_places(value):
        split = value.reshape(sp_frames, n_sp, n_tp, places, width)
        split = lax.dynamic_slice_in_dim(split, my_tp, 1, axis=2)[:, :, 0].transpose(1, 0, 2, 3)
        got = lax.all_to_all(split, "sp", 0, 0, tiled=True)
        if not zipped:
            got = got.reshape(all_frames, blocks, per_block, width).transpose(1, 0, 2, 3)
        return got.reshape(blocks * rows, width)

    def split_output(value):
        if not zipped:
            value = value.reshape(blocks, all_frames, per_block, width).transpose(1, 0, 2, 3)
        return lax.all_to_all(
            value.reshape(n_sp, sp_frames, places, width), "sp", 0, 0, tiled=True
        )

    step = 0
    while chain_s.steps or modulation.steps:
        chain_s.go()
        modulation.go()
        if step == LATE_STEP:
            late = stage([chain_s, modulation], late)
        else:
            stage([chain_s, modulation])
        step += 1
    late = lax.all_gather(late, ("tp", "sp"), axis=0).reshape(n_tp, n_sp, 3, row_sp, -1)
    if row_sp % 16:
        late_t = [late[:, :, 0].reshape(n_tp, width, -1)]
    else:
        late_t = [late]
    (modulation,) = modulation.state
    coarse = lax.reduce_precision(modulation, 8, 7)
    mst = jnp.concatenate([coarse, modulation - coarse]).astype(BF)
    mst_s, mst_t, mst_f = (mst[:, i * 3 * width : (i + 1) * 3 * width] for i in range(3))


    own = tokens.reshape(sp_frames, PATCHES, width)
    x1_shape = (devices, frames, places, width) if zipped else (frames, PATCHES, width)
    x1_frames, h1, qkv1, p1, o1, a1 = forward(
        meta_s, own, frames, PATCHES, hot_s, mst_s, None, chain_s.state, place, n_tp, heads,
        x1_shape, BF,
    )
    x1 = to_places(x1_frames)
    x1, grad_in = stage([], x1, grad_out)
    grad_rows = input_to_places(grad_in)
    x2, h2, qkv2, p2, o2, a2 = forward(
        meta0, x1, blocks, rows, hot_t, mst_t, keys, late_t, None, n_tp, heads, x1.shape, F32
    )

    feed_args = x2.reshape(blocks * rows, width), grad_rows, hot_f, hot_f_t, mst_f, late, masks
    if near:
        *sums, far_terms = feed_half(meta0, *feed_args, None)
        block_out, dx2, dm_f, near_terms = feed_half(meta0, *feed_args, sums)
        out_f = scatter([far_terms, near_terms], early=True)
        out_f.go()
        dx2, block_out = stage([out_f], dx2, block_out)
    else:
        *sums, up_one, down_one = feed_half(meta0, *feed_args, None)
        block_out, dx2, dm_f, up_two, down_two = feed_half(meta0, *feed_args, sums)
        pair = [scatter(p).run()[0] for p in ((up_one, up_two), (down_one, down_two))]
        out_f = Chain((jnp.concatenate(pair),), [])

    out_f.go()
    block_out = split_output(block_out)
    dx1, dm_t, *terms_t = backward(
        meta0, dx2.reshape(x2.shape), x1, hot_t, hot_t_t, mst_t, a2, h2, o2, qkv2, p2, late_t,
        place, masks, row_sp, heads,
    )
    dx1_frames = to_frames(dx1)
    block_out, terms_t = stage([out_f], block_out, terms_t)
    all_out = lax.all_gather(block_out, "tp", axis=0)
    out_t = scatter(terms_t, by_bits=True)
    out_f.go()
    out_f.go()
    out_t.go()
    dx1_frames = stage([out_t, out_f], dx1_frames)

    out_f.go()
    out_t.go()
    dqkv1, *terms_s = backward_grads(
        meta0, dx1_frames, hot_s, mst_s, h1, o1, qkv1, p1, chain_s.state, place, masks, row_sp, heads
    )
    dqkv1, terms_s, all_out = stage([out_t, out_f], dqkv1, terms_s, all_out)
    out_s = scatter(terms_s, direct=True)
    out_s.go()
    out_t.go()
    dqkv1 = stage([out_s, out_t], dqkv1)
    out_s.go()
    out_t.go()
    dx0, dm_s = input_back(
        meta_s, dx1_frames, own, hot_s, hot_s_t, mst_s, a1, dqkv1, chain_s.state, place, heads
    )
    dm = sum_chain(
        jnp.concatenate([dm_s, dm_t, dm_f], axis=-1), [(a, [b]) for a, b in reversed(far + last)]
    )
    for _ in range(DM_EARLY):
        dm.go()
    dx0, dm.state = stage([out_s, out_t], dx0, dm.state)

    grad_tokens = lax.all_gather(dx0, "tp", axis=0).reshape(-1, width)
    out_s.run()
    (dm,) = dm.run()
    sum_f, sum_t = out_f.run()[0], attention_grads(out_t.run()[0])
    sum_f = sum_f[:row_sp], sum_f[row_sp:].T
    all_out = all_out.transpose(2, 1, 0, 3, 4).reshape(-1, width)
    sum_t, sum_f, dm, all_out = stage([out_s], sum_t, sum_f, dm, all_out)
    low = dm.astype(BF)
    mine = jnp.dot(low, w_mod.T, preferred_element_type=F32)
    spot = jnp.arange(n_sp)[:, None, None] == my_sp
    part = sum_chain(jnp.where(spot, mine[None], 0.0), wide)
    part.run()
    grad_mod = jnp.dot(cond_rows.T, low, preferred_element_type=F32)
    grad_act = part.state[0].transpose(1, 0, 2).reshape(clips, width)
    unused, silu_pull = jax.vjp(jax.nn.silu, condition)
    grad_condition = silu_pull(grad_act)[0]
    sum_qs, sum_os = attention_grads(out_s.state[0])
    return (
        all_out,
        grad_tokens,
        grad_condition,
        grad_mod,
        sum_qs,
        sum_os,
        *sum_t,
        *sum_f,
    )


def solution(mesh):
    placed = (
        P("sp", None),
        P(),
        P(),
        P("sp", None),
        P(None, "sp", "tp"),
        P("tp", "sp"),
        P(None, "sp", "tp"),
        P("tp", "sp"),
        P("sp", "tp"),
        P("tp", "sp"),
        P("sp", None),
    )
    return jax.shard_map(
        shards,
        mesh=mesh,
        in_specs=placed,
        out_specs=(
            P("sp", None),
            P("sp", None),
            P(),
            P("sp", None),
            P(None, "sp", "tp"),
            P("tp", "sp"),
            P(None, "sp", "tp"),
            P("tp", "sp"),
            P("sp", "tp"),
            P("tp", "sp"),
        ),
        check_vma=False,
    )
```

```python
import functools

import jax
import jax.numpy as jnp
from jax import lax
from jax.experimental import pallas as pl
from jax.experimental.pallas import tpu as pltpu
from jax.sharding import PartitionSpec as P

HD = 64
PATCHES = 256
BLOCK_ROWS = 256
COSTS = (20, 20, 2, 1, 20)
LATE_STEP = -1
DM_EARLY = 0
EPSILON = 1e-06
HIGHEST = lax.Precision.HIGHEST
BF = jnp.bfloat16
F32 = jnp.float32


def bits_of(size):
    return size.bit_length() - 1


def swap(value, axis, bit):
    size = lax.axis_size(axis)
    return lax.ppermute(value, axis, [(i, i ^ (1 << bit)) for i in range(size)])


def swap_far(value, far, mask):
    axis = far[0][0]
    flip = sum(1 << bit for i, (a, bit) in enumerate(far) if mask >> i & 1)
    size = lax.axis_size(axis)
    return lax.ppermute(value, axis, [(i, i ^ flip) for i in range(size)])


def swap_both(value, one, two):
    sizes = lax.axis_size("tp"), lax.axis_size("sp")
    bits = dict([one, two])
    flip = (sizes[1] << bits["tp"]) ^ (1 << bits["sp"])
    return lax.ppermute(value, ("tp", "sp"), [(i, i ^ flip) for i in range(sizes[0] * sizes[1])])


def my_bit(axis, bit):
    return (lax.axis_index(axis) >> bit) & 1


def cube_sum(value, dims):
    for axis, bit in dims:
        value = value + swap(value, axis, bit)
    return value


def cube_gather(block, dims):
    held = block[None]
    for axis, bit in dims:
        other = swap(held, axis, bit)
        high = my_bit(axis, bit) == 1
        held = jnp.concatenate([jnp.where(high, other, held), jnp.where(high, held, other)])
    return held


def cube_scatter(parts, dims):
    for axis, bit in reversed(dims):
        half = parts.shape[0] // 2
        mine = my_bit(axis, bit)
        send = lax.dynamic_slice_in_dim(parts, (1 - mine) * half, half)
        keep = lax.dynamic_slice_in_dim(parts, mine * half, half)
        got = swap(send, axis, bit)
        parts = keep.astype(F32) + got.astype(F32)
        if half > 1:
            parts = parts.astype(BF)
    return parts[0]


def in_device_order(gathered, dims, back=False):
    count = len(dims)
    want = [("tp", b) for b in reversed(range(bits_of(lax.axis_size("tp"))))]
    want += [("sp", b) for b in reversed(range(bits_of(lax.axis_size("sp"))))]
    have = list(reversed(dims))
    tail = gathered.shape[1:]
    if back:
        have, want = want, have
    split = gathered.reshape((2,) * count + tail)
    order = [have.index(w) for w in want]
    split = split.transpose(order + [count + i for i in range(len(tail))])
    return split.reshape((2**count,) + tail)


VMEM_BYTES = 52 * 1024 * 1024


def cost(micros):
    return pl.CostEstimate(flops=micros * 10**9, bytes_accessed=2**10, transcendentals=0)


def after(value, *others):
    return lax.optimization_barrier((value,) + others)[0]


class Chain:
    def __init__(self, state, steps):
        self.state, self.steps = tuple(state), list(steps)

    def go(self):
        if self.steps:
            self.state = tuple(self.steps.pop(0)(*self.state))

    def run(self):
        while self.steps:
            self.go()
        return self.state


def stage(chains, *values):
    states, values = lax.optimization_barrier(([c.state for c in chains], values))
    for chain, state in zip(chains, states):
        chain.state = tuple(state)
    return values if len(values) != 1 else values[0]


def gather_chain(block, far, last):
    def far_step(held):
        return (jnp.concatenate([held] + [swap_far(held, far, m) for m in range(1, 1 << len(far))]),)

    def split(held):
        half = held.shape[1] // 2
        one, two = held[:, :half], held[:, half:]
        return (
            jnp.concatenate([one, swap(one, *last[0])]),
            jnp.concatenate([two, swap(two, *last[1])]),
        )

    def join(one, two):
        return (jnp.concatenate([one, swap(one, *last[1]), two, swap(two, *last[0])]),)

    def final(held):
        return (held, swap(held, *last[2]))

    return Chain((block[None],), [far_step, split, join, final])


def scatter_chain(other, mine, far, last, direct=False, early=False, by_bits=False):
    def add(left, *rights):
        return sum((r.astype(F32) for r in rights), left.astype(F32))

    def first(other, mine):
        total = add(mine, swap(other, *last[2])).astype(BF)
        count, rows = total.shape[0], total.shape[1]
        if direct:
            parts = total.reshape((2, 2, count // 4, rows) + total.shape[2:])
            return parts[0, 0], parts[0, 1], parts[1, 0], parts[1, 1]
        total = total.reshape((2, 2, count // 4, 2, rows // 2) + total.shape[2:])
        one, two = total[:, :, :, 0], total[:, :, :, 1]
        return one[0], one[1], two[:, 0], two[:, 1]

    def second(keep_one, send_one, keep_two, send_two):
        return keep_one, swap(send_one, *last[1]), keep_two, swap(send_two, *last[0])

    def second_sum(keep_one, got_one, keep_two, got_two):
        one = add(keep_one, got_one).astype(BF)
        two = add(keep_two, got_two).astype(BF)
        return one[0], one[1], two[0], two[1]

    def third(keep_one, send_one, keep_two, send_two):
        one = add(keep_one, swap(send_one, *last[0])).astype(BF)
        two = add(keep_two, swap(send_two, *last[1])).astype(BF)
        both = jnp.concatenate([one, two], axis=1)
        return tuple(both[m] for m in range(both.shape[0]))

    def at_once(keep, send_near, send_far, send_both):
        got = (
            swap(send_near, *last[0]),
            swap(send_far, *last[1]),
            swap_both(send_both, last[0], last[1]),
        )
        total = add(keep, *got).astype(BF)
        return tuple(total[m] for m in range(total.shape[0]))

    def far_step(*parts):
        return (add(parts[0], *[swap_far(p, far, m + 1) for m, p in enumerate(parts[1:])]),)

    def bit_step(bit):
        def run(*parts):
            half = len(parts) // 2
            sent = swap(jnp.stack(parts[half:]), *far[bit])
            sums = [add(p, g) for p, g in zip(parts[:half], sent)]
            return (sums[0],) if half == 1 else tuple(v.astype(BF) for v in sums)

        return run

    far_steps = [bit_step(b) for b in reversed(range(len(far)))] if by_bits else [far_step]

    def both_seconds(*state):
        return second_sum(*second(*state))

    if direct:
        steps = [first, at_once]
    elif early:
        steps = [first, second, second_sum, third]
    else:
        steps = [first, both_seconds, third]
    return Chain((other, mine), steps + far_steps)


def sum_chain(value, dims):
    def step(axis, bits):
        masks = [0]
        for bit in bits:
            masks += [m | 1 << bit for m in masks]
        size = lax.axis_size(axis)

        def run(value):
            others = [lax.ppermute(value, axis, [(i, i ^ m) for i in range(size)]) for m in masks[1:]]
            return (sum(others, value),)

        return run

    return Chain((value,), [step(*d) for d in dims])


def dims_masks(dims):
    masks = []
    for m in range(2 ** len(dims)):
        flip = {"tp": 0, "sp": 0}
        for place, (axis, bit) in enumerate(dims):
            flip[axis] |= ((m >> place) & 1) << bit
        masks.append((flip["tp"], flip["sp"]))
    return masks


def tp_flip(last, step):
    return (step % 2) << last[1][1] | (1 - step // 2) << last[2][1]


def tp_at(place, step, meta):
    if place is None:
        return step
    return meta[1] ^ tp_flip(place[1], step)


def dot(left, right, left_dim, right_dim):
    return lax.dot_general(
        left, right, (((left_dim,), (right_dim,)), ((), ())), preferred_element_type=F32
    )


def norm_rows(operand):
    centred = operand - jnp.mean(operand, axis=-1, keepdims=True)
    inverse = lax.rsqrt(jnp.mean(centred * centred, axis=-1, keepdims=True) + EPSILON)
    return (centred * inverse, inverse)


def norm_back(incoming, normed, inverse):
    first_mean = jnp.mean(incoming, axis=-1, keepdims=True)
    second_mean = jnp.mean(incoming * normed, axis=-1, keepdims=True)
    return inverse * (incoming - first_mean - normed * second_mean)


def params(count=1):
    return pltpu.CompilerParams(
        dimension_semantics=("arbitrary",) * count, vmem_limit_bytes=VMEM_BYTES
    )


def whole(shape):
    zeros = (0,) * len(shape)
    return pl.BlockSpec(shape, lambda g, meta: zeros, pipeline_mode=pl.Buffered(1))


def step_weights(meta, pieces, place, step, target):
    if place is None:
        return pieces[0]
    far, last = place
    near_count = 1 << len(far)
    half = pieces[0].shape[1]
    index = step % 2

    def fill(piece):
        for m in range(2 * near_count):
            z, y = m % near_count, m // near_count
            flip = sum(1 << bit for i, (a, bit) in enumerate(far) if z >> i & 1)
            flip |= y << last[0][1]
            at = pl.multiple_of((meta[2] ^ flip) * (2 * half), 2 * half)
            target[pl.ds(at, half), :] = piece[index * 2 * near_count + m]
            target[pl.ds(at + half, half), :] = piece[
                4 * near_count + y * 2 * near_count + index * near_count + z
            ]

    @pl.when(step // 2 == 1)
    def _():
        fill(pieces[0])

    @pl.when(step // 2 == 0)
    def _():
        fill(pieces[1])

    return target


def columns(weights, start, stop):
    if len(weights.shape) == 2:
        return weights[:, start:stop]
    if len(weights.shape) == 3:
        return weights[0, :, start:stop]
    return weights[0, :, 0, :, start:stop].reshape(-1, stop - start)


def split_places(pair):
    count, width = pair.shape[0], pair.shape[3]
    one, two = pair[:, 0], pair[:, 1]
    upper = lax.broadcasted_iota(jnp.int32, one.shape, 1) < 4
    left = jnp.where(upper, one, pltpu.roll(two, 4, 1))
    right = jnp.where(upper, pltpu.roll(one, 4, 1), two)
    return left.reshape(count * 8, width), right.reshape(count * 8, width)


def join_places(left, right):
    count, width = left.shape[0] // 8, left.shape[1]
    left, right = left.reshape(count, 8, width), right.reshape(count, 8, width)
    upper = lax.broadcasted_iota(jnp.int32, left.shape, 1) < 4
    one = jnp.where(upper, left, pltpu.roll(right, 4, 1))
    two = jnp.where(upper, pltpu.roll(left, 4, 1), right)
    return one, two


def blocks_of(x, groups):
    if len(x.shape) == 4 and groups == 2 and x.shape[1:3] == (2, 8):
        return list(split_places(x[...].astype(F32)))
    return [x[g].astype(F32) for g in range(groups)]


def forward_kernel(place, heads, masked, zipped, meta, x, hot, mst, key_r, key_c, *refs):
    pieces = refs[: 1 if place is None else 2]
    x_out, h_out, qkv_out, p_out, o_out, a_out, w, acc = refs[len(pieces) :]
    groups, rows, width = h_out.shape
    head_tp = heads * HD
    step = pl.program_id(0)

    def modulation(g, i):
        return dot(hot[g % hot.shape[0]], mst[:, i * width : (i + 1) * width], 1, 0)

    @pl.when(step == 0)
    def _():
        for g, xin in enumerate(blocks_of(x, groups)):
            normed = norm_rows(xin)[0]
            h_out[g] = (normed * (1.0 + modulation(g, 1)) + modulation(g, 0)).astype(BF)

    wt = step_weights(meta, pieces, place, step, w)
    bias = jnp.where(key_r[...] == key_c[...], 0.0, -1e30) if masked else None
    h = h_out[...].reshape(groups * rows, width)
    proj = dot(h, columns(wt, 0, 3 * head_tp), 1, 0).astype(BF)
    qkv_out[:, 0] = proj.reshape(groups, rows, 3 * head_tp)
    mixed = []
    for g in range(groups):
        outs = []
        for j in range(heads):
            q, k, v = (
                proj[g * rows : (g + 1) * rows, i * head_tp + j * HD : i * head_tp + (j + 1) * HD]
                for i in range(3)
            )
            scores = dot(k, q * jnp.asarray(0.125, BF), 1, 1)
            if masked:
                scores = scores + bias
            e = jnp.exp(scores - jnp.max(scores, axis=0, keepdims=True))
            p = (e * (1.0 / jnp.sum(e, axis=0, keepdims=True))).astype(BF)
            p_out[g, j] = p
            outs.append(dot(v, p, 0, 0))
        mixed.append(jnp.concatenate(outs, axis=0).T.astype(BF))
        o_out[g, 0] = mixed[-1]
    o = jnp.concatenate(mixed, axis=0)
    part = dot(o, columns(wt, 3 * head_tp, 4 * head_tp), 1, 1)

    @pl.when(step == 0)
    def _():
        acc[...] = part

    @pl.when(step > 0)
    def _():
        acc[...] += part

    @pl.when(step == pl.num_programs(0) - 1)
    def _():
        new = []
        for g, xin in enumerate(blocks_of(x, groups)):
            total = acc[g * rows : (g + 1) * rows, :]
            a_out[g] = total.astype(BF)
            new.append(xin + modulation(g, 2) * total)
        if zipped:
            one, two = join_places(*new)
            x_out[:, 0], x_out[:, 1] = one.astype(x_out.dtype), two.astype(x_out.dtype)
        else:
            for g in range(groups):
                if len(x_out.shape) == 4:
                    shape = (x_out.shape[0],) + x_out.shape[2:]
                    x_out[:, g] = new[g].reshape(shape).astype(x_out.dtype)
                else:
                    x_out[g] = new[g].astype(x_out.dtype)


def weight_specs(pieces, place):
    if place is not None:
        return [whole(p.shape) for p in pieces]
    (full,) = pieces
    if full.ndim == 5:
        block = (1, full.shape[1], 1) + full.shape[3:]
        return [pl.BlockSpec(block, lambda g, meta: (g, 0, 0, 0, 0))]
    return [pl.BlockSpec((1,) + full.shape[1:], lambda g, meta: (g, 0, 0))]


def head_spec(place, groups, *shape):
    zeros = (0,) * (len(shape) - 1)
    return pl.BlockSpec((groups,) + shape, lambda g, meta: (0, tp_at(place, g, meta)) + zeros)


def fixed(shape):
    zeros = (0,) * len(shape)
    return pl.BlockSpec(shape, lambda g, meta: zeros)


def rows_spec(x, groups, zipped):
    if zipped or x.ndim == 4:
        return whole(x.shape)
    return pl.BlockSpec(
        (groups,) + x.shape[1:], lambda g, meta: (meta[0] // groups, 0, 0),
        pipeline_mode=pl.Buffered(1),
    )


def forward(meta, x, groups, rows, hot, mst, keys, pieces, place, n_tp, heads, x_shape, out_dtype):
    width = x.shape[-1]
    lanes = 4 * heads * HD
    masked = keys is not None
    zipped = x.ndim == 4
    if keys is None:
        keys = jnp.zeros((8, 1), jnp.int32), jnp.zeros((1, 128), jnp.int32)
    return pl.pallas_call(
        functools.partial(forward_kernel, place, heads, masked, zipped),
        out_shape=[
            jax.ShapeDtypeStruct(x_shape, out_dtype),
            jax.ShapeDtypeStruct((groups, rows, width), BF),
            jax.ShapeDtypeStruct((groups, n_tp, rows, 3 * heads * HD), BF),
            jax.ShapeDtypeStruct((groups, n_tp * heads, rows, rows), BF),
            jax.ShapeDtypeStruct((groups, n_tp, rows, heads * HD), BF),
            jax.ShapeDtypeStruct((groups, rows, width), BF),
        ],
        grid_spec=pltpu.PrefetchScalarGridSpec(
            num_scalar_prefetch=1,
            grid=(n_tp,),
            in_specs=[
                rows_spec(x, groups, zipped),
                whole(hot.shape),
                whole(mst.shape),
                whole(keys[0].shape),
                whole(keys[1].shape),
            ]
            + weight_specs(pieces, place),
            out_specs=[
                fixed(x_shape),
                fixed((groups, rows, width)),
                head_spec(place, groups, 1, rows, 3 * heads * HD),
                head_spec(place, groups, heads, rows, rows),
                head_spec(place, groups, 1, rows, heads * HD),
                fixed((groups, rows, width)),
            ],
            scratch_shapes=[
                pltpu.VMEM((width, lanes), BF),
                pltpu.VMEM((groups * rows, width), F32),
            ],
        ),
        compiler_params=params(),
        cost_estimate=cost(COSTS[0]),
    )(meta, x, hot, mst, *keys, *pieces)


def grads_in(dx, groups, rows):
    if len(dx.shape) == 4 and dx.shape[1] == groups and dx.shape[0] * dx.shape[2] == rows:
        return [dx[:, g].astype(F32).reshape(rows, dx.shape[3]) for g in range(groups)]
    return [dx[g].astype(F32) for g in range(groups)]


def heads_back(heads, w, da, qkv, p, groups, rows):
    head_tp = heads * HD
    do = dot(da, columns(w, 3 * head_tp, 4 * head_tp), 1, 0).astype(BF)
    out = []
    for g in range(groups):
        got = [[], [], []]
        for j in range(heads):
            q, k, v = (
                qkv[g, 0, :, i * head_tp + j * HD : i * head_tp + (j + 1) * HD] for i in range(3)
            )
            dop = do[g * rows : (g + 1) * rows, j * HD : (j + 1) * HD]
            prob = p[g, j]
            dp = dot(v, dop, 1, 1)
            prob32 = prob.astype(F32)
            prod = prob32 * dp
            ds = (prod - prob32 * jnp.sum(prod, axis=0, keepdims=True)).astype(BF)
            got[0].append(dot(k, ds, 0, 0))
            got[1].append(dot(ds, q, 1, 0))
            got[2].append(dot(prob, dop, 1, 0))
        dq = jnp.concatenate(got[0], axis=0).T * 0.125
        dk = jnp.concatenate(got[1], axis=1) * 0.125
        out.append(jnp.concatenate([dq, dk] + got[2], axis=1).astype(BF))
    return out[0] if groups == 1 else jnp.concatenate(out, axis=0)


def finish_rows(hot, hot_t, mst, x, a, grads, dh, dm_out, groups):
    rows, width = a.shape[1], a.shape[2]
    sums = None
    out = []
    for g, xin in enumerate(blocks_of(x, groups)):
        at = slice(g * rows, (g + 1) * rows)
        gain = 1.0 + dot(hot[g % hot.shape[0]], mst[:, width : 2 * width], 1, 0)
        normed, inverse = norm_rows(xin)
        part = dh[at, :]
        grad = grads[g]
        out.append(grad + norm_back(part * gain, normed, inverse))
        new = [
            dot(hot_t[g % hot.shape[0]], value.astype(BF), 1, 0)
            for value in (part, part * normed, grad * a[g].astype(F32))
        ]
        sums = new if sums is None else [s + n for s, n in zip(sums, new)]
    for i in range(3):
        dm_out[:, i * width : (i + 1) * width] = sums[i]
    return out


def half_specs(half, shape):
    zeros = (0,) * len(shape)
    return [
        pl.BlockSpec((1,) + shape, lambda g, meta: (jnp.minimum(g, half - 1),) + zeros),
        pl.BlockSpec((1,) + shape, lambda g, meta: (jnp.maximum(g - half, 0),) + zeros),
    ]


def store_grads(masks, meta, step, first, second, blocks, outs):
    wide = first.shape[1]
    if masks is None:
        outs[0][0, :, :wide] = first
        outs[0][0, :, wide:] = second
        return
    blocks[:, :wide] = first
    blocks[:, wide:] = second
    half = pl.num_programs(0) // 2

    @pl.when(step < half)
    def _():
        store_blocks(meta, masks, blocks, outs[0].at[0])

    @pl.when(step >= half)
    def _():
        store_blocks(meta, masks, blocks, outs[1].at[0])


def grads_out(masks, n_tp, width, row_sp, lanes):
    if masks is None:
        out_shape = [jax.ShapeDtypeStruct((n_tp, width, lanes), BF)]
        return out_shape, [pl.BlockSpec((1, width, lanes), lambda g, meta: (g, 0, 0))]
    half = n_tp // 2
    shape = (len(masks) // n_tp, row_sp, lanes)
    return [jax.ShapeDtypeStruct((half,) + shape, BF)] * 2, half_specs(half, shape)


def back_kernel(masks, heads, meta, dx, x, hot, hot_t, mst, a, h, o, qkv, p, w, *refs):
    dx_out, dm_out, *outs, dh, h_t, da, da_t, blocks = refs
    groups, rows, width = a.shape
    head_tp = heads * HD
    step = pl.program_id(0)
    zipped = len(x.shape) == 4

    @pl.when(step == 0)
    def _():
        for g, grad in enumerate(blocks_of(dx, groups)):
            at = slice(g * rows, (g + 1) * rows)
            gate = dot(hot[g % hot.shape[0]], mst[:, 2 * width :], 1, 0)
            low = (gate * grad).astype(BF)
            da[at, :] = low
            da_t[:, at] = low.T
            h_t[:, at] = h[g].T

    dqkv = heads_back(heads, w, da[...], qkv, p, groups, rows)
    part = dot(dqkv, columns(w, 0, 3 * head_tp), 1, 1)
    first = dot(h_t[...], dqkv, 1, 0).astype(BF)
    second = dot(da_t[...], o[...].reshape(groups * rows, head_tp), 1, 0).astype(BF)
    store_grads(masks, meta, step, first, second, blocks, outs)

    @pl.when(step == 0)
    def _():
        dh[...] = part

    @pl.when(step > 0)
    def _():
        dh[...] += part

    @pl.when(step == pl.num_programs(0) - 1)
    def _():
        grads = blocks_of(dx, groups)
        new = finish_rows(hot, hot_t, mst, x, a, grads, dh, dm_out, groups)
        if zipped:
            one, two = join_places(*new)
            dx_out[:, 0], dx_out[:, 1] = one.astype(BF), two.astype(BF)
        else:
            for g in range(groups):
                dx_out[g] = new[g].astype(BF)


def backward(meta, dx, x, hot, hot_t, mst, a, h, o, qkv, p, pieces, place, masks, row_sp, heads):
    groups, n_tp, rows = qkv.shape[:3]
    width = a.shape[2]
    clips = hot_t.shape[1]
    lanes = 4 * heads * HD
    out_shape, out_specs = grads_out(masks, n_tp, width, row_sp, lanes)
    (full,) = pieces
    ahead = (1, full.shape[1], 1) if full.ndim == 5 else (1,)
    block = ahead + full.shape[-2:]
    zeros = (0,) * (len(block) - 1)
    return pl.pallas_call(
        functools.partial(back_kernel, masks, heads),
        out_shape=[
            jax.ShapeDtypeStruct(x.shape, BF),
            jax.ShapeDtypeStruct((clips, 3 * width), F32),
        ]
        + out_shape,
        grid_spec=pltpu.PrefetchScalarGridSpec(
            num_scalar_prefetch=1,
            grid=(n_tp,),
            in_specs=[
                whole(dx.shape),
                whole(x.shape),
                whole(hot.shape),
                whole(hot_t.shape),
                whole(mst.shape),
                whole(a.shape),
                whole(h.shape),
                head_spec(place, groups, 1, rows, heads * HD),
                head_spec(place, groups, 1, rows, 3 * heads * HD),
                head_spec(place, groups, heads, rows, rows),
                pl.BlockSpec(block, lambda g, meta: (tp_at(place, g, meta),) + zeros),
            ],
            out_specs=[fixed(x.shape), fixed((clips, 3 * width))] + out_specs,
            scratch_shapes=[
                pltpu.VMEM((groups * rows, width), F32),
                pltpu.VMEM((width, groups * rows), BF),
                pltpu.VMEM((groups * rows, width), BF),
                pltpu.VMEM((width, groups * rows), BF),
                pltpu.VMEM((width, lanes), BF),
            ],
        ),
        compiler_params=params(),
        cost_estimate=cost(COSTS[1]),
    )(meta, dx, x, hot, hot_t, mst, a, h, o, qkv, p, full)


def back_grads_kernel(place, masks, heads, meta, dx, hot, mst, h, o, qkv, p, *refs):
    pieces = refs[: 1 if place is None else 2]
    dqkv_out, *outs, w, h_t, da, da_t, blocks = refs[len(pieces) :]
    groups, rows, width = h.shape
    head_tp = heads * HD
    step = pl.program_id(0)

    @pl.when(step == 0)
    def _():
        for g, grad in enumerate(grads_in(dx, groups, rows)):
            at = slice(g * rows, (g + 1) * rows)
            gate = dot(hot[g % hot.shape[0]], mst[:, 2 * width :], 1, 0)
            low = (gate * grad).astype(BF)
            da[at, :] = low
            da_t[:, at] = low.T
            h_t[:, at] = h[g].T

    wt = step_weights(meta, pieces, place, step, w)
    dqkv = heads_back(heads, wt, da[...], qkv, p, groups, rows)
    dqkv_out[:, 0] = dqkv.reshape(groups, rows, 3 * head_tp)
    first = dot(h_t[...], dqkv, 1, 0).astype(BF)
    second = dot(da_t[...], o[...].reshape(groups * rows, head_tp), 1, 0).astype(BF)
    store_grads(masks, meta, step, first, second, blocks, outs)


def backward_grads(meta, dx, hot, mst, h, o, qkv, p, pieces, place, masks, row_sp, heads):
    groups, n_tp, rows = qkv.shape[:3]
    width = h.shape[2]
    lanes = 4 * heads * HD
    out_shape, out_specs = grads_out(masks, n_tp, width, row_sp, lanes)
    return pl.pallas_call(
        functools.partial(back_grads_kernel, place, masks, heads),
        out_shape=[jax.ShapeDtypeStruct(qkv.shape, BF)] + out_shape,
        grid_spec=pltpu.PrefetchScalarGridSpec(
            num_scalar_prefetch=1,
            grid=(n_tp,),
            in_specs=[
                whole(dx.shape),
                whole(hot.shape),
                whole(mst.shape),
                whole(h.shape),
                head_spec(place, groups, 1, rows, heads * HD),
                head_spec(place, groups, 1, rows, 3 * heads * HD),
                head_spec(place, groups, heads, rows, rows),
            ]
            + weight_specs(pieces, place),
            out_specs=[head_spec(place, groups, 1, rows, 3 * heads * HD)] + out_specs,
            scratch_shapes=[
                pltpu.VMEM((width, lanes), BF),
                pltpu.VMEM((width, groups * rows), BF),
                pltpu.VMEM((groups * rows, width), BF),
                pltpu.VMEM((width, groups * rows), BF),
                pltpu.VMEM((width, lanes), BF),
            ],
        ),
        compiler_params=params(),
        cost_estimate=cost(COSTS[1]),
    )(meta, dx, hot, mst, h, o, qkv, p, *pieces)


def input_back_kernel(place, heads, meta, dx, x, hot, hot_t, mst, a, dqkv, *refs):
    pieces = refs[: 1 if place is None else 2]
    dx_out, dm_out, w, dh = refs[len(pieces) :]
    groups, rows, width = a.shape
    head_tp = heads * HD
    step = pl.program_id(0)
    wt = step_weights(meta, pieces, place, step, w)
    all_rows = dqkv[...].reshape(groups * rows, 3 * head_tp)
    part = dot(all_rows, columns(wt, 0, 3 * head_tp), 1, 1)

    @pl.when(step == 0)
    def _():
        dh[...] = part

    @pl.when(step > 0)
    def _():
        dh[...] += part

    @pl.when(step == pl.num_programs(0) - 1)
    def _():
        grads = grads_in(dx, groups, rows)
        new = finish_rows(hot, hot_t, mst, x, a, grads, dh, dm_out, groups)
        for g in range(groups):
            dx_out[g] = new[g].astype(BF)


def input_back(meta, dx, x, hot, hot_t, mst, a, dqkv, pieces, place, heads):
    groups, n_tp, rows = dqkv.shape[:3]
    width = a.shape[2]
    clips = hot_t.shape[1]
    return pl.pallas_call(
        functools.partial(input_back_kernel, place, heads),
        out_shape=[
            jax.ShapeDtypeStruct(a.shape, BF),
            jax.ShapeDtypeStruct((clips, 3 * width), F32),
        ],
        grid_spec=pltpu.PrefetchScalarGridSpec(
            num_scalar_prefetch=1,
            grid=(n_tp,),
            in_specs=[
                whole(dx.shape),
                rows_spec(x, groups, False),
                whole(hot.shape),
                whole(hot_t.shape),
                whole(mst.shape),
                whole(a.shape),
                head_spec(place, groups, 1, rows, 3 * heads * HD),
            ]
            + weight_specs(pieces, place),
            out_specs=[fixed(a.shape), fixed((clips, 3 * width))],
            scratch_shapes=[
                pltpu.VMEM((width, 4 * heads * HD), BF),
                pltpu.VMEM((groups * rows, width), F32),
            ],
        ),
        compiler_params=params(),
        cost_estimate=cost(COSTS[4]),
    )(meta, dx, x, hot, hot_t, mst, a, dqkv, *pieces)


def store_blocks(meta, masks, scratch, target):
    count, rows = target.shape[0], target.shape[1]
    for place in range(count):
        at = pl.multiple_of((meta[2] ^ masks[place][1]) * rows, rows)
        target[place] = scratch[pl.ds(at, rows), :]


def tp_of(masks, n_tp, g, meta):
    if masks is None:
        return g
    flips = [masks[i * (len(masks) // n_tp)][0] for i in range(n_tp)]
    flips = flips[n_tp // 2 :] + flips[: n_tp // 2]
    flip = 0
    for i, value in enumerate(flips):
        flip = jnp.where(g == i, value, flip)
    return meta[1] ^ flip


GELU_A = 0.7978845608028654
GELU_B = 0.044715


def feed_kernel(masks, last_call, meta, x2, dy, hot, hot_t, mst, up, down, *refs):
    if last_call:
        acc_in, dh_in, out, dx_out, dm_out, *grads, h3, da3, h3_t, da3_t, acc, dh, blocks = refs
    else:
        acc, dh, *grads, h3, da3, h3_t, da3_t, blocks = refs
    width = x2.shape[1]
    step = pl.program_id(0)

    def modulation(i):
        return dot(hot[...], mst[:, i * width : (i + 1) * width], 1, 0)

    @pl.when(step == 0)
    def _():
        normed = norm_rows(x2[...])[0]
        h3[...] = (normed * (1.0 + modulation(1)) + modulation(0)).astype(BF)
        da3[...] = (modulation(2) * dy[...].astype(F32)).astype(BF)
        h3_t[...] = h3[...].T
        da3_t[...] = da3[...].T
        if last_call:
            acc[...], dh[...] = acc_in[...], dh_in[...]
        else:
            acc[...] = jnp.zeros_like(acc)
            dh[...] = jnp.zeros_like(dh)

    wu = up[...].reshape(width, -1)
    wd = down[...].reshape(width, -1)
    u = dot(h3[...], wu, 1, 0)
    square = u * u
    th = jnp.tanh(GELU_A * (u + GELU_B * (square * u)))
    g = (0.5 * u * (1.0 + th)).astype(BF)
    slope = 0.5 * (1.0 + th) + (0.5 * GELU_A) * u * (1.0 - th * th) * (
        1.0 + (3.0 * GELU_B) * square
    )
    dg = dot(da3[...], wd, 1, 0)
    du = (dg * slope).astype(BF)
    acc[...] += dot(g, wd, 1, 1)
    dh[...] += dot(du, wu, 1, 1)
    grad_up = dot(h3_t[...], du, 1, 0).astype(BF)
    grad_down = dot(da3_t[...], g, 1, 0).astype(BF)
    if masks is None:
        grads[0][0], grads[1][0] = grad_up, grad_down
    else:
        for i, value in enumerate((grad_up, grad_down)):
            blocks[...] = value
            store_blocks(meta, masks, blocks, grads[0].at[0, :, i])

    if last_call:

        @pl.when(step == pl.num_programs(0) - 1)
        def _():
            grad = dy[...].astype(F32)
            a3 = acc[...]
            xin = x2[...]
            normed, inverse = norm_rows(xin)
            out[...] = (xin + modulation(2) * a3).astype(BF)
            dh3 = dh[...]
            dx_out[...] = grad + norm_back(dh3 * (1.0 + modulation(1)), normed, inverse)
            for i, value in enumerate([dh3, dh3 * normed, grad * a3]):
                dm_out[:, i * width : (i + 1) * width] = dot(hot_t[...], value.astype(BF), 1, 0)


def feed_half(meta, x2, dy, hot, hot_t, mst, weights, masks, sums):
    rows, width = x2.shape
    n_tp, n_sp, unused, row_sp, units = weights.shape
    clips = hot_t.shape[0]
    half = n_tp // 2
    last_call = sums is not None
    start = half if last_call else 0
    at = lambda g, meta: tp_of(masks, n_tp, g + start, meta)
    if masks is None:
        blocked = weights.transpose(2, 0, 1, 3, 4).reshape(3, n_tp, width, units)
        up, down = blocked[1], blocked[2]
        specs = [pl.BlockSpec((1, width, units), lambda g, meta: (g + start, 0, 0))] * 2
        grad_shapes = [(half, width, units)] * 2
    else:
        up = down = weights
        specs = [
            pl.BlockSpec(
                (1, n_sp, 1, row_sp, units), lambda g, meta, i=i: (at(g, meta), 0, i, 0, 0)
            )
            for i in (1, 2)
        ]
        grad_shapes = [(half, n_sp, 2, row_sp, units)]
    zeros = (0,) * (len(grad_shapes[0]) - 1)
    grad_spec = pl.BlockSpec((1,) + grad_shapes[0][1:], lambda g, meta: (g,) + zeros)
    plain = lambda s: pl.BlockSpec(s, lambda g, meta: (0, 0))
    total = pltpu.VMEM((rows, width), F32)
    kept = [pltpu.VMEM((rows, width), BF)] * 2 + [pltpu.VMEM((width, rows), BF)] * 2
    if last_call:
        out_types = [((rows, width), BF), ((rows, width), F32), ((clips, 3 * width), F32)]
        scratch = kept + [total, total]
    else:
        out_types = [((rows, width), F32), ((rows, width), F32)]
        scratch = kept
    return pl.pallas_call(
        functools.partial(feed_kernel, masks, last_call),
        out_shape=[jax.ShapeDtypeStruct(*t) for t in out_types]
        + [jax.ShapeDtypeStruct(g, BF) for g in grad_shapes],
        grid_spec=pltpu.PrefetchScalarGridSpec(
            num_scalar_prefetch=1,
            grid=(half,),
            in_specs=[
                whole(x2.shape),
                whole(dy.shape),
                whole(hot.shape),
                whole(hot_t.shape),
                whole(mst.shape),
            ]
            + specs
            + ([whole(x2.shape)] * 2 if last_call else []),
            out_specs=[plain(t[0]) for t in out_types] + [grad_spec] * len(grad_shapes),
            scratch_shapes=scratch + [pltpu.VMEM((width, units), BF)],
        ),
        compiler_params=params(),
        cost_estimate=cost(COSTS[3]),
    )(meta, x2, dy, hot, hot_t, mst, up, down, *(sums or ()))


def shards(
    tokens, condition, clip_ids, w_mod, w_qkv_s, w_o_s, w_qkv_t, w_o_t, w_up, w_down, grad_out
):
    n_tp, n_sp = lax.axis_size("tp"), lax.axis_size("sp")
    devices = n_tp * n_sp
    my_tp, my_sp = lax.axis_index("tp"), lax.axis_index("sp")
    width = tokens.shape[1]
    sp_frames = tokens.shape[0] // PATCHES
    frames = sp_frames // n_tp
    all_frames = sp_frames * n_sp
    places = PATCHES // devices
    per_block = max(1, min(places, BLOCK_ROWS // all_frames))
    blocks = places // per_block
    rows = all_frames * per_block
    clips = condition.shape[0]
    head_tp = w_o_s.shape[0]
    heads = head_tp // HD
    row_sp = w_up.shape[0]
    zipped = (frames, per_block, blocks) == (2, 4, 2)

    sp_bits = bits_of(n_sp)
    tp_bits = bits_of(n_tp)
    far = [("sp", b) for b in reversed(range(1, sp_bits))]
    last = [("sp", 0), ("tp", 1), ("tp", 0)]
    every = [("tp", b) for b in range(tp_bits)] + [("sp", b) for b in range(sp_bits)]
    sp_dims = [("sp", b) for b in range(sp_bits)]
    near = row_sp % 32 == 0

    def pack(w_qkv, w_o):
        flat = w_qkv.transpose(1, 0, 2).reshape(row_sp, -1)
        return jnp.concatenate([flat, w_o.T], axis=1)

    masks = dims_masks(far + last) if near else None

    def scatter(terms, **how):
        if near:
            other, mine = (v.reshape((devices // 2, -1) + v.shape[-1:]) for v in terms)
            return scatter_chain(other, mine, far, last, **how)
        terms = jnp.concatenate(terms)
        terms = terms.reshape((devices, -1) + terms.shape[-1:])
        terms = in_device_order(terms, far + last, back=True)
        return Chain((terms,), [lambda v: (cube_scatter(v, far + last),)])

    def attention_grads(mine):
        mine = mine.reshape(row_sp, 4, head_tp)
        return mine[:, :3].transpose(1, 0, 2), mine[:, 3].T

    def gather(block):
        if near:
            return gather_chain(block, far, last)
        dims = far + last

        def run(block):
            full = in_device_order(cube_gather(block, dims), dims)
            return (full.reshape(n_tp, width, -1),)

        return Chain((block,), [run])

    cond_act = jax.nn.silu(condition).astype(BF)
    cond_rows = lax.dynamic_slice_in_dim(cond_act, my_sp * row_sp, row_sp, axis=1)
    wide = [("sp", [0]), ("sp", list(range(1, sp_bits)))] if near else [("sp", [b]) for a, b in sp_dims]
    modulation = sum_chain(jnp.dot(cond_rows, w_mod, preferred_element_type=F32), wide)
    place = (far, last) if near else None
    chain_s = gather(pack(w_qkv_s, w_o_s))
    late = jnp.stack([pack(w_qkv_t, w_o_t), w_up, w_down.T])

    def hot_of(ids):
        hot = (ids[..., None] == jnp.arange(clips, dtype=jnp.int32)).astype(BF)
        return jnp.concatenate([hot, hot], axis=-1), jnp.swapaxes(hot, -1, -2)

    first = my_sp * sp_frames + my_tp * frames
    ids_s = lax.dynamic_slice_in_dim(clip_ids, first, frames)
    hot_s, hot_s_t = hot_of(jnp.repeat(ids_s[:, None], PATCHES, axis=1))
    ids_t = jnp.repeat(clip_ids, per_block)
    hot_t, hot_t_t = hot_of(ids_t[None])
    hot_f, hot_f_t = hot_of(
        jnp.repeat(clip_ids, places) if zipped else jnp.tile(ids_t, blocks)
    )
    key = ids_t * per_block + jnp.tile(jnp.arange(per_block, dtype=jnp.int32), all_frames)
    keys = key[:, None], key[None, :]
    meta0 = jnp.stack([0 * my_tp, my_tp, my_sp]).astype(jnp.int32)
    meta_s = jnp.stack([my_tp * frames, my_tp, my_sp]).astype(jnp.int32)

    def exchange(value):
        return lax.all_to_all(value, ("sp", "tp"), 0, 0, tiled=True)

    def to_places(value):
        if zipped:
            return exchange(value)
        split = value.reshape(frames, devices, blocks, per_block, width).transpose(1, 2, 0, 3, 4)
        return exchange(split).transpose(1, 0, 2, 3, 4).reshape(blocks, rows, width)

    def to_frames(value):
        if zipped:
            return exchange(value)
        split = value.reshape(blocks, devices, frames, per_block, width).transpose(1, 0, 2, 3, 4)
        return exchange(split).transpose(2, 0, 1, 3, 4).reshape(frames, PATCHES, width)

    def input_to_places(value):
        split = value.reshape(sp_frames, n_sp, n_tp, places, width)
        split = lax.dynamic_slice_in_dim(split, my_tp, 1, axis=2)[:, :, 0].transpose(1, 0, 2, 3)
        got = lax.all_to_all(split, "sp", 0, 0, tiled=True)
        if not zipped:
            got = got.reshape(all_frames, blocks, per_block, width).transpose(1, 0, 2, 3)
        return got.reshape(blocks * rows, width)

    def split_output(value):
        if not zipped:
            value = value.reshape(blocks, all_frames, per_block, width).transpose(1, 0, 2, 3)
        return lax.all_to_all(
            value.reshape(n_sp, sp_frames, places, width), "sp", 0, 0, tiled=True
        )

    step = 0
    while chain_s.steps or modulation.steps:
        chain_s.go()
        modulation.go()
        if step == LATE_STEP:
            late = stage([chain_s, modulation], late)
        else:
            stage([chain_s, modulation])
        step += 1
    late = lax.all_gather(late, ("tp", "sp"), axis=0).reshape(n_tp, n_sp, 3, row_sp, -1)
    if row_sp % 16:
        late_t = [late[:, :, 0].reshape(n_tp, width, -1)]
    else:
        late_t = [late]
    (modulation,) = modulation.state
    coarse = lax.reduce_precision(modulation, 8, 7)
    mst = jnp.concatenate([coarse, modulation - coarse]).astype(BF)
    mst_s, mst_t, mst_f = (mst[:, i * 3 * width : (i + 1) * 3 * width] for i in range(3))


    own = tokens.reshape(sp_frames, PATCHES, width)
    x1_shape = (devices, frames, places, width) if zipped else (frames, PATCHES, width)
    x1_frames, h1, qkv1, p1, o1, a1 = forward(
        meta_s, own, frames, PATCHES, hot_s, mst_s, None, chain_s.state, place, n_tp, heads,
        x1_shape, BF,
    )
    grad_rows = input_to_places(after(grad_out, *chain_s.state))
    x1 = to_places(x1_frames)
    x1, grad_rows = stage([], x1, grad_rows)
    x2, h2, qkv2, p2, o2, a2 = forward(
        meta0, x1, blocks, rows, hot_t, mst_t, keys, late_t, None, n_tp, heads, x1.shape, F32
    )

    feed_args = x2.reshape(blocks * rows, width), grad_rows, hot_f, hot_f_t, mst_f, late, masks
    if near:
        *sums, far_terms = feed_half(meta0, *feed_args, None)
        block_out, dx2, dm_f, near_terms = feed_half(meta0, *feed_args, sums)
        out_f = scatter([far_terms, near_terms], early=True)
        out_f.go()
        dx2, block_out = stage([out_f], dx2, block_out)
    else:
        *sums, up_one, down_one = feed_half(meta0, *feed_args, None)
        block_out, dx2, dm_f, up_two, down_two = feed_half(meta0, *feed_args, sums)
        pair = [scatter(p).run()[0] for p in ((up_one, up_two), (down_one, down_two))]
        out_f = Chain((jnp.concatenate(pair),), [])

    out_f.go()
    block_out = split_output(block_out)
    dx1, dm_t, *terms_t = backward(
        meta0, dx2.reshape(x2.shape), x1, hot_t, hot_t_t, mst_t, a2, h2, o2, qkv2, p2, late_t,
        place, masks, row_sp, heads,
    )
    dx1_frames = to_frames(dx1)
    block_out, terms_t = stage([out_f], block_out, terms_t)
    all_out = lax.all_gather(block_out, "tp", axis=0)
    out_t = scatter(terms_t, by_bits=True)
    out_f.go()
    out_f.go()
    out_t.go()
    dx1_frames = stage([out_t, out_f], dx1_frames)

    out_f.go()
    out_t.go()
    dqkv1, *terms_s = backward_grads(
        meta0, dx1_frames, hot_s, mst_s, h1, o1, qkv1, p1, chain_s.state, place, masks, row_sp, heads
    )
    dqkv1, terms_s, all_out = stage([out_t, out_f], dqkv1, terms_s, all_out)
    out_s = scatter(terms_s, direct=True)
    out_s.go()
    out_t.go()
    dqkv1 = stage([out_s, out_t], dqkv1)
    out_s.go()
    out_t.go()
    dx0, dm_s = input_back(
        meta_s, dx1_frames, own, hot_s, hot_s_t, mst_s, a1, dqkv1, chain_s.state, place, heads
    )
    dm = sum_chain(
        jnp.concatenate([dm_s, dm_t, dm_f], axis=-1), [(a, [b]) for a, b in reversed(far + last)]
    )
    for _ in range(DM_EARLY):
        dm.go()
    dx0, dm.state = stage([out_s, out_t], dx0, dm.state)

    grad_tokens = lax.all_gather(dx0, "tp", axis=0).reshape(-1, width)
    out_s.run()
    (dm,) = dm.run()
    sum_f, sum_t = out_f.run()[0], attention_grads(out_t.run()[0])
    sum_f = sum_f[:row_sp], sum_f[row_sp:].T
    all_out = all_out.transpose(2, 1, 0, 3, 4).reshape(-1, width)
    sum_t, sum_f, dm, all_out = stage([out_s], sum_t, sum_f, dm, all_out)
    low = dm.astype(BF)
    mine = jnp.dot(low, w_mod.T, preferred_element_type=F32)
    spot = jnp.arange(n_sp)[:, None, None] == my_sp
    part = sum_chain(jnp.where(spot, mine[None], 0.0), wide)
    part.run()
    grad_mod = jnp.dot(cond_rows.T, low, preferred_element_type=F32)
    grad_act = part.state[0].transpose(1, 0, 2).reshape(clips, width)
    unused, silu_pull = jax.vjp(jax.nn.silu, condition)
    grad_condition = silu_pull(grad_act)[0]
    sum_qs, sum_os = attention_grads(out_s.state[0])
    return (
        all_out,
        grad_tokens,
        grad_condition,
        grad_mod,
        sum_qs,
        sum_os,
        *sum_t,
        *sum_f,
    )


def solution(mesh):
    placed = (
        P("sp", None),
        P(),
        P(),
        P("sp", None),
        P(None, "sp", "tp"),
        P("tp", "sp"),
        P(None, "sp", "tp"),
        P("tp", "sp"),
        P("sp", "tp"),
        P("tp", "sp"),
        P("sp", None),
    )
    return jax.shard_map(
        shards,
        mesh=mesh,
        in_specs=placed,
        out_specs=(
            P("sp", None),
            P("sp", None),
            P(),
            P("sp", None),
            P(None, "sp", "tp"),
            P("tp", "sp"),
            P(None, "sp", "tp"),
            P("tp", "sp"),
            P("sp", "tp"),
            P("tp", "sp"),
        ),
        check_vma=False,
    )
```
